128 devices in a mesh: leaf: 8 (over y, core), front: 16 (over z, x).
Axes of the slice: x: 4, y: 4, z: 4, core: 2. Of those that a mesh axis runs over, the one named last changes fastest.
Arguments:
- front_entries: float32 [16, 8, 128, 8, 16, 128], P(None, 'leaf', None, None, 'front'), as said below
- child_panels: bfloat16 [8, 2048, 512], P('leaf', 'front'), may hold values from -0.053955078 to 0.053955078
- child_blocks: bfloat16 [8, 2048, 2048], P('leaf', None, 'front'), as said below
- child_map: int32 [8, 16], replicated, may hold values from 0 to 127, as said below
Outputs:
- factored: float32 [16, 8, 128, 8, 16, 128], P(None, 'leaf', None, None, 'front')
The draws below stay inside these ranges and needn't reach their ends.
Inputs may be any that keep to these rules, and one draw needn't show every extreme that they name: The blocks of one subtree go to distinct parent blocks, and child_map[c, j] modulo 16 equals j. front_entries is symmetric and positive definite, with its diagonal in 6 to 9. `child_blocks`: each subtree's block is symmetric with diagonal in 6 to 9 and small independent entries elsewhere.
All inputs are finite; a program needn't handle non-finite values.
Results may differ from the reference program's by a relative error of at most 0.0012.
Values may be sent and summed in bfloat16 or wider, within the bound.
No kernel may reach another device: no remote copies, remote signals or barrier semaphores. Data moves between devices by JAX's collectives and lax.ppermute only.
A program may use at most 128 MiB of HBM per device.

```python
import jax
import jax.numpy as jnp
from jax import lax

BLK = 128
PIV = 512
KS = 8
NBP = 128
KU = 16
NU = 2048
N_LEAF = 8
N_FRONT = 16


def draw_front_entries(key, part):
    order = BLK * NBP
    split = KS * BLK
    horizontal = jax.random.uniform(jax.random.fold_in(key, 11), (order,), jnp.float32, 0.0, 1.0)
    vertical = jax.random.uniform(jax.random.fold_in(key, 12), (order,), jnp.float32, 0.0, 1.0)
    diagonal = jax.random.uniform(jax.random.fold_in(key, 13), (order,), jnp.float32, 5.0, 8.0)
    position = jnp.arange(order, dtype=jnp.int32)
    amplitude = 4.0 * 3.0 ** 0.5 / ((order - split) ** 0.5 + split ** 0.5)
    coupling = jax.random.uniform(jax.random.fold_in(key, 15), (order - split, split), jnp.float32, -amplitude, amplitude)
    left_part = jnp.concatenate([jnp.zeros((split, split), jnp.float32), coupling], axis=0)

    def one_block(inputs):
        block_horizontal, block_vertical, block_diagonal, block_position = inputs
        first_gap = block_horizontal[:, None] - horizontal[None, :]
        second_gap = block_vertical[:, None] - vertical[None, :]
        distance = jnp.sqrt(first_gap * first_gap + second_gap * second_gap)
        kernel = jnp.exp(-distance / 0.12)
        own_rows = jnp.take(left_part, block_position, axis=0)
        own_rows = jnp.concatenate([own_rows, jnp.zeros((block_position.shape[0], order - split), jnp.float32)], axis=1)
        mirrored = jnp.take(left_part, jnp.minimum(block_position, split - 1), axis=1).T
        mirrored = jnp.where(block_position[:, None] < split, mirrored, 0.0)
        kernel = kernel + own_rows + mirrored
        return jnp.where(block_position[:, None] == position[None, :], kernel + block_diagonal[:, None], kernel)
    row_blocks = lax.map(one_block, (horizontal.reshape(NBP, BLK), vertical.reshape(NBP, BLK), diagonal.reshape(NBP, BLK), position.reshape(NBP, BLK)))
    return row_blocks.reshape(NBP // N_LEAF, N_LEAF, BLK, NBP // N_FRONT, N_FRONT, BLK)


def draw_child_blocks(key, part):
    spread = 0.95 / NU ** 0.5
    noise = jax.random.uniform(jax.random.fold_in(key, 21), (N_LEAF, NU, NU), jnp.float32, -spread, spread)
    noise = (noise + jnp.swapaxes(noise, 1, 2)) * 0.5
    diagonal = jax.random.uniform(jax.random.fold_in(key, 22), (N_LEAF, NU), jnp.float32, 6.0, 9.0)
    index = jnp.arange(NU)
    same = index[:, None] == index[None, :]
    return jnp.where(same[None, :, :], diagonal[:, None, :], noise).astype(jnp.bfloat16)


def draw_child_map(key, part):
    cycles = jax.random.randint(jax.random.fold_in(key, 31), (N_LEAF, KU), 0, NBP // N_FRONT)
    cycles = cycles.at[0, 0].set(0)
    cycles = cycles.at[0, KU - 1].set(NBP // N_FRONT - 1)
    return (jnp.arange(KU, dtype=jnp.int32)[None, :] + N_FRONT * cycles).astype(jnp.int32)


def levels(stream_key, dims, cuts, low, high):
    factor_of, own = 1.0, jax.random.fold_in(stream_key, 6)
    for axis_at, shards_of in cuts:
        heights = jnp.exp(jax.random.uniform(jax.random.fold_in(own, axis_at), (shards_of,), jnp.float32, low / len(cuts), high / len(cuts)))
        factor_of = factor_of * jnp.repeat(heights, dims[axis_at] // shards_of).reshape([-1 if axis == axis_at else 1 for axis in range(len(dims))])
    return factor_of


def setup_inputs(seed: int = 0) -> dict:
    key_of = jax.random.split(jax.random.key(seed), 5)
    return {
        "front_entries": draw_front_entries(jax.random.fold_in(key_of[4], 71), 0),
        "child_panels": jnp.clip(jax.random.uniform(key_of[1], (N_LEAF, NU, PIV), jnp.float32, -0.053955078, 0.053955078) * levels(key_of[1], (N_LEAF, NU, PIV), ((0, 8), (1, 16)), -0.4, 0.0), -0.053955078, 0.053955078).astype(jnp.bfloat16),
        "child_blocks": draw_child_blocks(jax.random.fold_in(key_of[4], 71), 0),
        "child_map": draw_child_map(jax.random.fold_in(key_of[4], 71), 0),
    }


def reference(front_entries, child_panels, child_blocks, child_map):
    order = BLK * NBP
    assembled = front_entries.reshape(order, order)
    offsets = jnp.arange(BLK, dtype=jnp.int32)
    for child in range(N_LEAF):
        panel = child_panels[child]
        update = (child_blocks[child].astype(jnp.float32) - jnp.dot(panel.astype(jnp.float32), panel.T.astype(jnp.float32), preferred_element_type=jnp.float32)).astype(jnp.bfloat16)
        update = lax.optimization_barrier(update).astype(jnp.float32)
        places = (child_map[child][:, None] * BLK + offsets[None, :]).reshape(-1).astype(jnp.int32)
        assembled = assembled.at[places[:, None], places[None, :]].add(update)
    split = KS * BLK
    lower11 = jnp.linalg.cholesky(assembled[:split, :split])
    lower21 = lax.linalg.triangular_solve(lower11, assembled[split:, :split], left_side=False, lower=True, transpose_a=True)
    schur = assembled[split:, split:] - jnp.dot(lower21.astype(jnp.float32), lower21.T.astype(jnp.float32), precision=lax.Precision.HIGHEST, preferred_element_type=jnp.float32)
    result = jnp.zeros((order, order), jnp.float32)
    result = result.at[:split, :split].set(jnp.tril(lower11))
    result = result.at[split:, :split].set(lower21)
    result = result.at[split:, split:].set(schur)
    return result.reshape(NBP // N_LEAF, N_LEAF, BLK, NBP // N_FRONT, N_FRONT, BLK)
```

```python
import jax
import jax.numpy as jnp
from jax import lax
from jax.experimental import pallas as pl
from jax.experimental.pallas import tpu as pltpu
from jax.sharding import PartitionSpec as P

F32 = jnp.float32
BF16 = jnp.bfloat16
KS = 8
BLK = 128
ORDER = KS * BLK
N_LEAF = 8
N_FRONT = 16
STEP_ROWS = 4
WHOLE = pl.BlockSpec(memory_space=pltpu.VMEM)
TABLE = pl.BlockSpec(memory_space=pltpu.SMEM)


def dot(a, b, ca, cb, precision=None):
    return lax.dot_general(
        a, b, (((ca,), (cb,)), ((), ())), precision=precision, preferred_element_type=F32
    )


def exact_dot(a, b, ca, cb):
    return dot(a, b, ca, cb, lax.Precision.HIGHEST)


def update_kernel(panels_ref, own_ref, block_ref, out_ref):
    own = own_ref[...]
    for block in range(N_FRONT):
        product = dot(panels_ref[block], own, 1, 1)
        given = block_ref[block * BLK : (block + 1) * BLK, :].astype(F32)
        out_ref[block % N_LEAF, block // N_LEAF] = (given - product).astype(BF16)


def updates(panels, own, block):
    return pl.pallas_call(
        update_kernel,
        name="updates",
        out_shape=jax.ShapeDtypeStruct((N_LEAF, 2, BLK, BLK), BF16),
        in_specs=[WHOLE] * 3,
        out_specs=WHOLE,
    )(panels, own, block)


def pivot_kernel(map_ref, front_ref, update_ref, flat_ref, turned_ref, first_ref, sum_ref):
    leaf = lax.axis_index("leaf")
    front = lax.axis_index("front")
    for s in range(8):
        sum_ref[:, s * BLK : (s + 1) * BLK] = front_ref[0, :, s, :]
    for c in range(N_LEAF):
        cycle = map_ref[c, front] // N_FRONT

        @pl.when(map_ref[c, leaf] // N_FRONT == 0)
        def _():
            cols = pl.ds(pl.multiple_of(cycle * BLK, BLK), BLK)
            sum_ref[:, cols] += update_ref[c, 0].astype(F32)

    first_ref[...] = sum_ref[:, :BLK].astype(BF16)
    flat_ref[...] = sum_ref[...].astype(BF16)
    for s in range(8):
        turned_ref[s] = jnp.transpose(sum_ref[:, s * BLK : (s + 1) * BLK]).astype(BF16)


def pivot_rows(child_map, front, received):
    return pl.pallas_call(
        pivot_kernel,
        name="pivot_rows",
        grid=(1,),
        out_shape=(
            jax.ShapeDtypeStruct((BLK, 8 * BLK), BF16),
            jax.ShapeDtypeStruct((8, BLK, BLK), BF16),
            jax.ShapeDtypeStruct((BLK, BLK), BF16),
        ),
        in_specs=[
            TABLE,
            pl.BlockSpec((1, BLK, 8, BLK), lambda i: (0, 0, 0, 0)),
            pl.BlockSpec((N_LEAF, 1, BLK, BLK), lambda i: (0, 0, 0, 0)),
        ],
        out_specs=(
            pl.BlockSpec((BLK, 8 * BLK), lambda i: (0, 0)),
            pl.BlockSpec((8, BLK, BLK), lambda i: (0, 0, 0)),
            pl.BlockSpec((BLK, BLK), lambda i: (0, 0)),
        ),
        scratch_shapes=[pltpu.VMEM((BLK, 8 * BLK), F32)],
    )(child_map, front, received)


def lanes(x, j):
    return jnp.broadcast_to(x[:, j : j + 1], (8, BLK))


def subs(x, i):
    return jnp.broadcast_to(x[i : i + 1, :], (8, BLK))


def sum_products(v, r):
    t = [v[i] * r[i] for i in range(8)]
    while len(t) > 1:
        t = [t[i] + t[i + 1] for i in range(0, len(t), 2)]
    return t[0]


def factor(g_ref, e_ref):
    for p in range(16):
        rows = pl.ds(8 * p, 8)
        below = pl.ds(8 * p + 8, 8)
        top = g_ref[rows, :]
        side = e_ref[rows, :]
        cols = [lanes(top, 8 * p + j) for j in range(8)]
        a = [[subs(cols[j], i) if j <= i else None for j in range(8)] for i in range(8)]
        r = [subs(top, i) for i in range(8)]
        e = [subs(side, i) for i in range(8)]
        more = p < 15
        if more:
            after = g_ref[below, :]
            v = [lanes(after, 8 * p + j) for j in range(8)]
        for j in range(8):
            inv = lax.rsqrt(a[j][j])
            r[j] = r[j] * inv
            e[j] = e[j] * inv
            if more:
                v[j] = v[j] * inv
            col = [None] * 8
            for i in range(j + 1, 8):
                col[i] = a[i][j] * inv
            for i in range(j + 1, 8):
                for k in range(j + 1, i + 1):
                    a[i][k] = a[i][k] - col[i] * col[k]
            for i in range(j + 1, 8):
                r[i] = r[i] - col[i] * r[j]
                e[i] = e[i] - col[i] * e[j]
                if more:
                    v[i] = v[i] - col[i] * v[j]
        if more:
            g_ref[below, :] = after - sum_products(v, r)
            e_ref[below, :] = e_ref[below, :] - sum_products(v, e)
        sub = lax.broadcasted_iota(jnp.int32, (8, BLK), 0)
        u, w = r[0], e[0]
        for i in range(1, 8):
            u = jnp.where(sub == i, r[i], u)
            w = jnp.where(sub == i, e[i], w)
        g_ref[rows, :] = u
        e_ref[rows, :] = w
        if p < 14:
            turned = jnp.transpose(u)
            for g in range(p + 2, 16):
                vg = [lanes(turned[8 * g : 8 * g + 8, :], i) for i in range(8)]
                there = pl.ds(8 * g, 8)
                g_ref[there, :] = g_ref[there, :] - sum_products(vg, r)
                e_ref[there, :] = e_ref[there, :] - sum_products(vg, e)


def cholesky_kernel(a_ref, hi_ref, lo_ref, l_ref, s_ref, d_ref, g_ref, e_ref):
    s_ref[...] = a_ref[...].astype(F32)
    row_id = lax.broadcasted_iota(jnp.int32, (BLK, BLK), 0)
    col_id = lax.broadcasted_iota(jnp.int32, (BLK, BLK), 1)
    ident = (row_id == col_id).astype(F32)

    @pl.loop(0, KS)
    def _(k):
        here = pl.ds(pl.multiple_of(k * BLK, BLK), BLK)
        g_ref[...] = s_ref[here, here]
        e_ref[...] = ident
        factor(g_ref, e_ref)
        d_ref[here, :] = g_ref[...]
        s_ref[here, here] = ident
        s_ref[here, :] = exact_dot(e_ref[...], s_ref[here, :], 1, 0)

        @pl.loop(k + 1, KS)
        def _(i):
            there = pl.ds(pl.multiple_of(i * BLK, BLK), BLK)
            s_ref[there, here] = jnp.zeros((BLK, BLK), F32)
            s_ref[there, :] = s_ref[there, :] - exact_dot(s_ref[here, there], s_ref[here, :], 0, 0)

    @pl.loop(0, KS)
    def _(k):
        here = pl.ds(pl.multiple_of(k * BLK, BLK), BLK)
        keep = lax.broadcasted_iota(jnp.int32, (BLK, ORDER), 1) < (k + 1) * BLK
        m = jnp.where(keep, s_ref[here, :], 0.0)
        hi = m.astype(BF16)
        hi_ref[here, :] = hi
        lo_ref[here, :] = (m - hi.astype(F32)).astype(BF16)

    leaf = lax.axis_index("leaf")
    front = jnp.minimum(lax.axis_index("front"), KS - 1)
    mine = pl.ds(pl.multiple_of(leaf * BLK, BLK), BLK)
    other = pl.ds(pl.multiple_of(front * BLK, BLK), BLK)
    upper = jnp.where(row_id <= col_id, d_ref[mine, :], 0.0)
    beyond = jnp.where(front < leaf, s_ref[other, mine], 0.0)
    l_ref[...] = jnp.transpose(jnp.where(front == leaf, upper, beyond))


def cholesky(a):
    return pl.pallas_call(
        cholesky_kernel,
        name="cholesky",
        out_shape=(
            jax.ShapeDtypeStruct((ORDER, ORDER), BF16),
            jax.ShapeDtypeStruct((ORDER, ORDER), BF16),
            jax.ShapeDtypeStruct((BLK, BLK), F32),
        ),
        in_specs=[WHOLE],
        out_specs=(WHOLE,) * 3,
        scratch_shapes=[
            pltpu.VMEM((ORDER, ORDER), F32),
            pltpu.VMEM((ORDER, BLK), F32),
            pltpu.VMEM((BLK, BLK), F32),
            pltpu.VMEM((BLK, BLK), F32),
        ],
        compiler_params=pltpu.CompilerParams(vmem_limit_bytes=24 << 20),
        cost_estimate=pl.CostEstimate(
            flops=60_000_000_000, bytes_accessed=6 << 20, transcendentals=1024
        ),
    )(a)


def schur_kernel(
    map_ref, hi_ref, lo_ref, cols_ref, l_ref, update_ref, rows_hbm, front_ref, out_ref,
    rows_ref, w_ref, low_ref, p_ref, sem
):
    step = pl.program_id(0)
    leaf = lax.axis_index("leaf")
    front = lax.axis_index("front")
    owner = jnp.minimum(front, KS - 1)
    rows_here = STEP_ROWS * BLK

    def fetch(b, a):
        return pltpu.make_async_copy(
            rows_hbm.at[b, a], rows_ref.at[b, :, :, pl.ds(a * BLK, BLK)], sem.at[b, a]
        )

    @pl.when(step == 0)
    def _():
        for b in range(2):
            for a in range(KS):
                fetch(b, a).start()
        for n in range(4):
            take = slice(n * 256, (n + 1) * 256)
            upto = slice(0, (n + 1) * 256)
            part = dot(hi_ref[take, upto], cols_ref[upto, :], 1, 0)
            part += dot(lo_ref[take, upto], cols_ref[upto, :], 1, 0)
            w_ref[take, :] = part.astype(BF16)
        for b in range(2):
            for a in range(KS):
                fetch(b, a).wait()

    for n in range(4):
        take = slice(n * 256, (n + 1) * 256)
        upto = slice(0, (n + 1) * 256)
        for q in range(STEP_ROWS):
            rows = rows_ref[q % 2, step * (STEP_ROWS // 2) + q // 2, :, upto]
            part = dot(rows, hi_ref[take, upto], 1, 1)
            part += dot(rows, lo_ref[take, upto], 1, 1)
            low_ref[q * BLK : (q + 1) * BLK, take] = part
    p_ref[...] = dot(low_ref[...].astype(BF16), w_ref[...], 1, 0)
    for c in range(N_LEAF):
        cols = pl.ds(pl.multiple_of(map_ref[c, front] // N_FRONT * BLK, BLK), BLK)
        for b in range(2):
            q = map_ref[c, leaf + b * N_LEAF] // N_FRONT * 2 + b - step * STEP_ROWS

            @pl.when((q >= 0) & (q < STEP_ROWS))
            def _():
                there = pl.ds(pl.multiple_of(q * BLK, BLK), BLK)
                p_ref[there, cols] = p_ref[there, cols] - update_ref[c, b].astype(F32)

    for q in range(STEP_ROWS):
        rows = slice(q * BLK, (q + 1) * BLK)
        for s in range(8):
            out_ref[q, :, s, :] = front_ref[q, :, s, :] - p_ref[rows, s * BLK : (s + 1) * BLK]

    @pl.when(front < KS)
    def _():
        column = pl.ds(pl.multiple_of(owner * BLK, BLK), BLK)
        for q in range(STEP_ROWS):
            out_ref[q, :, 0, :] = low_ref[q * BLK : (q + 1) * BLK, column]

    @pl.when(step == 0)
    def _():
        out_ref[0] = jnp.zeros((BLK, 8, BLK), F32)

        @pl.when(front < KS)
        def _():
            out_ref[0, :, 0, :] = l_ref[...]


def schur(child_map, hi, lo, cols, lower, received, rows, front):
    steps = 16 // STEP_ROWS
    block = pl.BlockSpec((STEP_ROWS, BLK, 8, BLK), lambda i: (i, 0, 0, 0))
    return pl.pallas_call(
        schur_kernel,
        name="schur",
        grid=(steps,),
        out_shape=jax.ShapeDtypeStruct((16, BLK, 8, BLK), F32),
        in_specs=[TABLE] + [WHOLE] * 5 + [pl.BlockSpec(memory_space=pl.ANY), block],
        out_specs=block,
        scratch_shapes=[
            pltpu.VMEM((2, 8, BLK, ORDER), BF16),
            pltpu.VMEM((ORDER, ORDER), BF16),
            pltpu.VMEM((STEP_ROWS * BLK, ORDER), F32),
            pltpu.VMEM((STEP_ROWS * BLK, ORDER), F32),
            pltpu.SemaphoreType.DMA((2, KS)),
        ],
        compiler_params=pltpu.CompilerParams(vmem_limit_bytes=48 << 20),
    )(child_map, hi, lo, cols, lower, received, rows, front)


def gather(x, axis, count):
    spread = jnp.broadcast_to(x[None], (count, *x.shape))
    return lax.all_to_all(spread, axis, 0, 0)


def on_device(front_entries, child_panels, child_blocks, child_map):
    front = front_entries.reshape(16, BLK, 8, BLK)
    panels = gather(child_panels[0], "front", N_FRONT)
    update = updates(panels, child_panels[0], child_blocks[0])
    received = lax.all_to_all(update, "leaf", 0, 0)
    flat, turned, first = pivot_rows(child_map, front, received)
    first_rows = gather(first, "front", N_FRONT)[:KS]
    first_rows = first_rows.transpose(1, 0, 2).reshape(BLK, ORDER)
    separator = gather(first_rows, "leaf", N_LEAF).reshape(ORDER, ORDER)
    swap = [
        (a * N_FRONT + b * N_LEAF + c, c * N_FRONT + b * N_LEAF + a)
        for a in range(N_LEAF)
        for b in range(2)
        for c in range(N_LEAF)
    ]
    cols = lax.all_gather(flat, "leaf", axis=0, tiled=True)
    rows = lax.all_gather(lax.ppermute(turned, ("leaf", "front"), swap), "front", axis=0)
    hi, lo, lower = cholesky(separator)
    out = schur(
        child_map, hi, lo, cols, lower, received, rows.reshape(2, KS, 8, BLK, BLK), front
    )
    return out.reshape(16, 1, BLK, 8, 1, BLK)


def solution(mesh):
    placed = (
        P(None, "leaf", None, None, "front", None),
        P("leaf", "front", None),
        P("leaf", None, "front"),
        P(),
    )
    return jax.shard_map(
        on_device,
        mesh=mesh,
        in_specs=placed,
        out_specs=P(None, "leaf", None, None, "front", None),
        check_vma=False,
    )
```

```python
import jax
import jax.numpy as jnp
from jax import lax
from jax.experimental import pallas as pl
from jax.experimental.pallas import tpu as pltpu
from jax.sharding import PartitionSpec as P

F32 = jnp.float32
BF16 = jnp.bfloat16
KS = 8
BLK = 128
ORDER = KS * BLK
N_LEAF = 8
N_FRONT = 16
STEP_ROWS = 4
MESH_AXES = ("leaf", "front")
WHOLE = pl.BlockSpec(memory_space=pltpu.VMEM)
TABLE = pl.BlockSpec(memory_space=pltpu.SMEM)


def dot(a, b, ca, cb, precision=None):
    return lax.dot_general(
        a, b, (((ca,), (cb,)), ((), ())), precision=precision, preferred_element_type=F32
    )


def exact_dot(a, b, ca, cb):
    return dot(a, b, ca, cb, lax.Precision.HIGHEST)


def place():
    return lax.axis_index("leaf"), lax.axis_index("front")


def rows_of(rows_ref, c):
    return jnp.concatenate([rows_ref[0, c], rows_ref[1, c]], axis=0)


def update_of(given, left, right):
    return (given.astype(F32) - dot(left, right, 1, 1)).astype(BF16)


def pivot_kernel(
    map_ref, front_ref, given_ref, rows_ref, cols_ref, flat_ref, turned_ref, first_ref, sum_ref
):
    leaf, front = place()
    for s in range(8):
        sum_ref[:, s * BLK : (s + 1) * BLK] = front_ref[pl.ds(s, BLK, stride=8), :]
    for c in range(N_LEAF):
        cycle = map_ref[c, front] // N_FRONT

        @pl.when(map_ref[c, leaf] // N_FRONT == 0)
        def _():
            cols = pl.ds(pl.multiple_of(cycle * BLK, BLK), BLK)
            update = update_of(given_ref[c, 0], rows_of(rows_ref, c), cols_ref[c])
            sum_ref[:, cols] += update.astype(F32)

    flat_ref[...] = sum_ref[...].astype(BF16)
    for s in range(8):
        turned_ref[s] = jnp.transpose(sum_ref[:, s * BLK : (s + 1) * BLK]).astype(BF16)
    half = BLK // 2
    bottom = sum_ref[half:, :BLK]
    top = jnp.where(leaf > front, jnp.transpose(sum_ref[:, :BLK])[:half], sum_ref[:half, :BLK])
    first_ref[0] = jnp.where(leaf < front, bottom, top).astype(BF16)
    first_ref[1] = bottom.astype(BF16)


def pivot_rows(child_map, front, given, rows, cols):
    return pl.pallas_call(
        pivot_kernel,
        name="pivot_rows",
        grid=(1,),
        out_shape=(
            jax.ShapeDtypeStruct((BLK, 8 * BLK), BF16),
            jax.ShapeDtypeStruct((8, BLK, BLK), BF16),
            jax.ShapeDtypeStruct((2, BLK // 2, BLK), BF16),
        ),
        in_specs=[
            TABLE,
            pl.BlockSpec((8 * BLK, BLK), lambda i: (0, 0)),
            pl.BlockSpec((N_LEAF, 1, BLK, BLK), lambda i: (0, 0, 0, 0)),
            pl.BlockSpec(rows.shape, lambda i: (0, 0, 0, 0)),
            pl.BlockSpec(cols.shape, lambda i: (0, 0, 0)),
        ],
        out_specs=(
            pl.BlockSpec((BLK, 8 * BLK), lambda i: (0, 0)),
            pl.BlockSpec((8, BLK, BLK), lambda i: (0, 0, 0)),
            pl.BlockSpec((2, BLK // 2, BLK), lambda i: (0, 0, 0)),
        ),
        scratch_shapes=[pltpu.VMEM((BLK, 8 * BLK), F32)],
    )(child_map, front, given, rows, cols)


def lanes(x, j):
    return jnp.broadcast_to(x[:, j : j + 1], (8, BLK))


def subs(x, i):
    return jnp.broadcast_to(x[i : i + 1, :], (8, BLK))


def sum_products(v, r):
    t = [v[i] * r[i] for i in range(8)]
    while len(t) > 1:
        t = [t[i] + t[i + 1] for i in range(0, len(t), 2)]
    return t[0]


def factor(g_ref, e_ref):
    for p in range(16):
        rows = pl.ds(8 * p, 8)
        below = pl.ds(8 * p + 8, 8)
        top = g_ref[rows, :]
        side = e_ref[rows, :]
        cols = [lanes(top, 8 * p + j) for j in range(8)]
        a = [[subs(cols[j], i) if j <= i else None for j in range(8)] for i in range(8)]
        r = [subs(top, i) for i in range(8)]
        e = [subs(side, i) for i in range(8)]
        more = p < 15
        if more:
            after = g_ref[below, :]
            v = [lanes(after, 8 * p + j) for j in range(8)]
        for j in range(8):
            inv = lax.rsqrt(a[j][j])
            r[j] = r[j] * inv
            e[j] = e[j] * inv
            if more:
                v[j] = v[j] * inv
            col = [None] * 8
            for i in range(j + 1, 8):
                col[i] = a[i][j] * inv
            for i in range(j + 1, 8):
                for k in range(j + 1, i + 1):
                    a[i][k] = a[i][k] - col[i] * col[k]
            for i in range(j + 1, 8):
                r[i] = r[i] - col[i] * r[j]
                e[i] = e[i] - col[i] * e[j]
                if more:
                    v[i] = v[i] - col[i] * v[j]
        if more:
            g_ref[below, :] = after - sum_products(v, r)
            e_ref[below, :] = e_ref[below, :] - sum_products(v, e)
        sub = lax.broadcasted_iota(jnp.int32, (8, BLK), 0)
        u, w = r[0], e[0]
        for i in range(1, 8):
            u = jnp.where(sub == i, r[i], u)
            w = jnp.where(sub == i, e[i], w)
        g_ref[rows, :] = u
        e_ref[rows, :] = w
        if p < 14:
            turned = jnp.transpose(u)
            for g in range(p + 2, 16):
                vg = [lanes(turned[8 * g : 8 * g + 8, :], i) for i in range(8)]
                there = pl.ds(8 * g, 8)
                g_ref[there, :] = g_ref[there, :] - sum_products(vg, r)
                e_ref[there, :] = e_ref[there, :] - sum_products(vg, e)


def halves(x):
    high = x.astype(BF16)
    return high, (x - high.astype(F32)).astype(BF16)


def dot3(a, b, ca, cb):
    return dot(a[0], b[0], ca, cb) + (dot(a[0], b[1], ca, cb) + dot(a[1], b[0], ca, cb))


def cholesky_kernel(a_ref, m_ref, l_ref, s_ref, d_ref, g_ref, e_ref, nh_ref, nl_ref):
    half = BLK // 2
    for r in range(KS):
        for c in range(r, KS):
            cols = slice(c * BLK, (c + 1) * BLK)
            lower = a_ref[r, KS] if c == r else a_ref[r, c]
            s_ref[r * BLK : r * BLK + half, cols] = a_ref[c, r].astype(F32)
            s_ref[r * BLK + half : (r + 1) * BLK, cols] = lower.astype(F32)
    row_id = lax.broadcasted_iota(jnp.int32, (BLK, BLK), 0)
    col_id = lax.broadcasted_iota(jnp.int32, (BLK, BLK), 1)
    ident = (row_id == col_id).astype(F32)

    @pl.loop(0, KS)
    def _(k):
        here = pl.ds(pl.multiple_of(k * BLK, BLK), BLK)
        g_ref[...] = s_ref[here, here]
        e_ref[...] = ident
        factor(g_ref, e_ref)
        d_ref[here, :] = g_ref[...]
        s_ref[here, here] = ident
        row = dot3(halves(e_ref[...]), halves(s_ref[here, :]), 1, 0)
        s_ref[here, :] = row
        nh_ref[...], nl_ref[...] = halves(row)

        @pl.loop(k + 1, KS)
        def _(i):
            there = pl.ds(pl.multiple_of(i * BLK, BLK), BLK)
            s_ref[there, here] = jnp.zeros((BLK, BLK), F32)
            part = nh_ref[:, there], nl_ref[:, there]
            s_ref[there, :] = s_ref[there, :] - dot3(part, (nh_ref[...], nl_ref[...]), 0, 0)

    @pl.loop(0, KS)
    def _(k):
        here = pl.ds(pl.multiple_of(k * BLK, BLK), BLK)
        keep = lax.broadcasted_iota(jnp.int32, (BLK, ORDER), 1) < (k + 1) * BLK
        m = jnp.where(keep, s_ref[here, :], 0.0)
        m_ref[here, :] = m.astype(BF16)

    leaf, front = place()
    front = jnp.minimum(front, KS - 1)
    mine = pl.ds(pl.multiple_of(leaf * BLK, BLK), BLK)
    other = pl.ds(pl.multiple_of(front * BLK, BLK), BLK)
    upper = jnp.where(row_id <= col_id, d_ref[mine, :], 0.0)
    beyond = jnp.where(front < leaf, s_ref[other, mine], 0.0)
    l_ref[...] = jnp.transpose(jnp.where(front == leaf, upper, beyond))


def cholesky(a):
    return pl.pallas_call(
        cholesky_kernel,
        name="cholesky",
        out_shape=(
            jax.ShapeDtypeStruct((ORDER, ORDER), BF16),
            jax.ShapeDtypeStruct((BLK, BLK), F32),
        ),
        in_specs=[WHOLE],
        out_specs=(WHOLE,) * 2,
        scratch_shapes=[
            pltpu.VMEM((ORDER, ORDER), F32),
            pltpu.VMEM((ORDER, BLK), F32),
            pltpu.VMEM((BLK, BLK), F32),
            pltpu.VMEM((BLK, BLK), F32),
            pltpu.VMEM((BLK, ORDER), BF16),
            pltpu.VMEM((BLK, ORDER), BF16),
        ],
        compiler_params=pltpu.CompilerParams(vmem_limit_bytes=24 << 20),
        cost_estimate=pl.CostEstimate(
            flops=60_000_000_000, bytes_accessed=6 << 20, transcendentals=1024
        ),
    )(a)


def schur_kernel(
    map_ref, m_ref, cols_ref, l_ref, given_ref, upper_ref, lower_ref, panel_ref, rows_hbm,
    front_ref, out_ref, rows_ref, w_ref, low_ref, p_ref, update_ref, sem
):
    step = pl.program_id(0)
    leaf = lax.axis_index("leaf")
    front = lax.axis_index("front")
    owner = jnp.minimum(front, KS - 1)
    rows_here = STEP_ROWS * BLK

    def fetch(b, a):
        return pltpu.make_async_copy(
            rows_hbm.at[b, a], rows_ref.at[b, :, :, pl.ds(a * BLK, BLK)], sem.at[b, a]
        )

    @pl.when(step == 0)
    def _():
        for b in range(2):
            for a in range(KS):
                fetch(b, a).start()
        for c in range(N_LEAF):
            update_ref[c, 0] = update_of(given_ref[c, 0], rows_of(upper_ref, c), panel_ref[c])
            update_ref[c, 1] = update_of(given_ref[c, 1], rows_of(lower_ref, c), panel_ref[c])
        for n in range(4):
            take = slice(n * 256, (n + 1) * 256)
            upto = slice(0, (n + 1) * 256)
            w_ref[take, :] = dot(m_ref[take, upto], cols_ref[upto, :], 1, 0).astype(BF16)
        for b in range(2):
            for a in range(KS):
                fetch(b, a).wait()

    for n in range(4):
        take = slice(n * 256, (n + 1) * 256)
        upto = slice(0, (n + 1) * 256)
        for q in range(STEP_ROWS):
            rows = rows_ref[q % 2, step * (STEP_ROWS // 2) + q // 2, :, upto]
            low_ref[q * BLK : (q + 1) * BLK, take] = dot(rows, m_ref[take, upto], 1, 1)
    p_ref[...] = dot(low_ref[...].astype(BF16), w_ref[...], 1, 0)
    for c in range(N_LEAF):
        cols = pl.ds(pl.multiple_of(map_ref[c, front] // N_FRONT * BLK, BLK), BLK)
        for b in range(2):
            q = map_ref[c, leaf + b * N_LEAF] // N_FRONT * 2 + b - step * STEP_ROWS

            @pl.when((q >= 0) & (q < STEP_ROWS))
            def _():
                there = pl.ds(pl.multiple_of(q * BLK, BLK), BLK)
                p_ref[there, cols] = p_ref[there, cols] - update_ref[c, b].astype(F32)

    for s in range(8):
        there = pl.ds(s, rows_here, stride=8)
        out_ref[there, :] = front_ref[there, :] - p_ref[:, s * BLK : (s + 1) * BLK]

    @pl.when(front < KS)
    def _():
        column = pl.ds(pl.multiple_of(owner * BLK, BLK), BLK)
        out_ref[pl.ds(0, rows_here, stride=8), :] = low_ref[:, column]

    @pl.when(step == 0)
    def _():
        out_ref[: 8 * BLK, :] = jnp.zeros((8 * BLK, BLK), F32)

        @pl.when(front < KS)
        def _():
            out_ref[pl.ds(0, BLK, stride=8), :] = l_ref[...]


def schur(child_map, m, cols, low, given, upper, lower, panels, rows, front):
    steps = 16 // STEP_ROWS
    block = pl.BlockSpec((STEP_ROWS * BLK * 8, BLK), lambda i: (i, 0))
    return pl.pallas_call(
        schur_kernel,
        name="schur",
        grid=(steps,),
        out_shape=jax.ShapeDtypeStruct((16 * BLK * 8, BLK), F32),
        in_specs=[TABLE] + [WHOLE] * 7 + [pl.BlockSpec(memory_space=pl.ANY), block],
        out_specs=block,
        scratch_shapes=[
            pltpu.VMEM((2, 8, BLK, ORDER), BF16),
            pltpu.VMEM((ORDER, ORDER), BF16),
            pltpu.VMEM((STEP_ROWS * BLK, ORDER), F32),
            pltpu.VMEM((STEP_ROWS * BLK, ORDER), F32),
            pltpu.VMEM((N_LEAF, 2, BLK, BLK), BF16),
            pltpu.SemaphoreType.DMA((2, KS)),
        ],
        compiler_params=pltpu.CompilerParams(vmem_limit_bytes=48 << 20),
    )(child_map, m, cols, low, given, upper, lower, panels, rows, front)


def gather(x, axis, count):
    spread = jnp.broadcast_to(x[None], (count, *x.shape))
    return lax.all_to_all(spread, axis, 0, 0)


def exchange(flip):
    return [
        (a * N_FRONT + b * N_LEAF + c, c * N_FRONT + (b ^ flip) * N_LEAF + a)
        for a in range(N_LEAF)
        for b in range(2)
        for c in range(N_LEAF)
    ]


def on_device(front_entries, child_panels, child_blocks, child_map):
    front = front_entries.reshape(16 * BLK * 8, BLK)
    front_id = lax.axis_index("front")
    leaf_id = lax.axis_index("leaf")
    own = child_panels[0]
    panels = lax.all_gather(own, "leaf", axis=0)
    halves_of = own.reshape(2, BLK // 2, own.shape[1])
    early = front_id < N_LEAF
    same = lax.ppermute(jnp.where(early, halves_of[0], halves_of[1]), MESH_AXES, exchange(0))
    other = lax.ppermute(jnp.where(early, halves_of[1], halves_of[0]), MESH_AXES, exchange(1))
    blocks = child_blocks[0].reshape(2, N_LEAF, BLK, BLK).transpose(1, 0, 2, 3)
    given = lax.all_to_all(blocks, "leaf", 0, 0)
    upper = gather(jnp.where(early, same, other), "front", N_FRONT)
    lower = lax.all_gather(jnp.where(early, other, same), "front", axis=0)
    shape = (2, N_LEAF, BLK // 2, own.shape[1])
    upper, lower = upper.reshape(shape), lower.reshape(shape)
    flat, turned, first = pivot_rows(child_map, front, given, upper, panels)
    pieces = gather(first, "front", N_FRONT)[:KS]
    extra = lax.dynamic_index_in_dim(pieces[:, 1], leaf_id, 0, keepdims=True)
    separator = gather(jnp.concatenate([pieces[:, 0], extra], axis=0), "leaf", N_LEAF)
    cols = lax.all_gather(flat, "leaf", axis=0, tiled=True)
    rows = lax.all_gather(lax.ppermute(turned, MESH_AXES, exchange(0)), "front", axis=0)
    m, low = cholesky(separator)
    rows = rows.reshape(2, KS, 8, BLK, BLK)
    out = schur(child_map, m, cols, low, given, upper, lower, panels, rows, front)
    return out.reshape(16, 1, BLK, 8, 1, BLK)


def solution(mesh):
    placed = (
        P(None, "leaf", None, None, "front", None),
        P("leaf", "front", None),
        P("leaf", None, "front"),
        P(),
    )
    return jax.shard_map(
        on_device,
        mesh=mesh,
        in_specs=placed,
        out_specs=P(None, "leaf", None, None, "front", None),
        check_vma=False,
    )
```

```python
import jax
import jax.numpy as jnp
from jax import lax
from jax.experimental import pallas as pl
from jax.experimental.pallas import tpu as pltpu
from jax.sharding import PartitionSpec as P


F32 = jnp.float32
BF16 = jnp.bfloat16
KS = 8
BLK = 128
ORDER = KS * BLK
N_LEAF = 8
N_FRONT = 16
STEP_ROWS = 4
MESH_AXES = ("leaf", "front")
WHOLE = pl.BlockSpec(memory_space=pltpu.VMEM)
TABLE = pl.BlockSpec(memory_space=pltpu.SMEM)


def dot(a, b, ca, cb, precision=None):
    return lax.dot_general(
        a, b, (((ca,), (cb,)), ((), ())), precision=precision, preferred_element_type=F32
    )


def place():
    return lax.axis_index("leaf"), lax.axis_index("front")


def rows_of(rows_ref, c):
    return jnp.concatenate([rows_ref[0, c], rows_ref[1, c]], axis=0)


def update_of(given, left, right):
    return (given.astype(F32) - dot(left, right, 1, 1)).astype(BF16)


def pivot_kernel(
    map_ref, front_ref, given_ref, rows_ref, cols_ref, flat_ref, turned_ref, first_ref, sum_ref
):
    leaf, front = place()
    for s in range(8):
        sum_ref[:, s * BLK : (s + 1) * BLK] = front_ref[pl.ds(s, BLK, stride=8), :]
    for c in range(N_LEAF):
        cycle = map_ref[c, front] // N_FRONT

        @pl.when(map_ref[c, leaf] // N_FRONT == 0)
        def _():
            cols = pl.ds(pl.multiple_of(cycle * BLK, BLK), BLK)
            update = update_of(given_ref[c, 0], rows_of(rows_ref, c), cols_ref[c])
            sum_ref[:, cols] += update.astype(F32)

    flat_ref[...] = sum_ref[...].astype(BF16)
    for s in range(8):
        turned_ref[s] = jnp.transpose(sum_ref[:, s * BLK : (s + 1) * BLK]).astype(BF16)
    half = BLK // 2
    bottom = sum_ref[half:, :BLK]
    top = jnp.where(leaf > front, jnp.transpose(sum_ref[:, :BLK])[:half], sum_ref[:half, :BLK])
    first_ref[0] = jnp.where(leaf < front, bottom, top).astype(BF16)
    first_ref[1] = bottom.astype(BF16)


def pivot_rows(child_map, front, given, rows, cols):
    return pl.pallas_call(
        pivot_kernel,
        name="pivot_rows",
        grid=(1,),
        out_shape=(
            jax.ShapeDtypeStruct((BLK, 8 * BLK), BF16),
            jax.ShapeDtypeStruct((8, BLK, BLK), BF16),
            jax.ShapeDtypeStruct((2, BLK // 2, BLK), BF16),
        ),
        in_specs=[
            TABLE,
            pl.BlockSpec((8 * BLK, BLK), lambda i: (0, 0)),
            pl.BlockSpec((N_LEAF, 1, BLK, BLK), lambda i: (0, 0, 0, 0)),
            pl.BlockSpec(rows.shape, lambda i: (0, 0, 0, 0)),
            pl.BlockSpec(cols.shape, lambda i: (0, 0, 0)),
        ],
        out_specs=(
            pl.BlockSpec((BLK, 8 * BLK), lambda i: (0, 0)),
            pl.BlockSpec((8, BLK, BLK), lambda i: (0, 0, 0)),
            pl.BlockSpec((2, BLK // 2, BLK), lambda i: (0, 0, 0)),
        ),
        scratch_shapes=[pltpu.VMEM((BLK, 8 * BLK), F32)],
    )(child_map, front, given, rows, cols)


def lanes(x, j):
    return jnp.broadcast_to(x[:, j : j + 1], (8, BLK))


def subs(x, i):
    return jnp.broadcast_to(x[i : i + 1, :], (8, BLK))


def sum_products(v, r):
    t = [v[i] * r[i] for i in range(8)]
    while len(t) > 1:
        t = [t[i] + t[i + 1] for i in range(0, len(t), 2)]
    return t[0]


def factor(g_ref, e_ref):
    for p in range(16):
        rows = pl.ds(8 * p, 8)
        below = pl.ds(8 * p + 8, 8)
        top = g_ref[rows, :]
        side = e_ref[rows, :]
        cols = [lanes(top, 8 * p + j) for j in range(8)]
        a = [[subs(cols[j], i) if j <= i else None for j in range(8)] for i in range(8)]
        r = [subs(top, i) for i in range(8)]
        e = [subs(side, i) for i in range(8)]
        more = p < 15
        if more:
            after = g_ref[below, :]
            v = [lanes(after, 8 * p + j) for j in range(8)]
        for j in range(8):
            inv = lax.rsqrt(a[j][j])
            r[j] = r[j] * inv
            e[j] = e[j] * inv
            if more:
                v[j] = v[j] * inv
            col = [None] * 8
            for i in range(j + 1, 8):
                col[i] = a[i][j] * inv
            for i in range(j + 1, 8):
                for k in range(j + 1, i + 1):
                    a[i][k] = a[i][k] - col[i] * col[k]
            for i in range(j + 1, 8):
                r[i] = r[i] - col[i] * r[j]
                e[i] = e[i] - col[i] * e[j]
                if more:
                    v[i] = v[i] - col[i] * v[j]
        if more:
            g_ref[below, :] = after - sum_products(v, r)
            e_ref[below, :] = e_ref[below, :] - sum_products(v, e)
        sub = lax.broadcasted_iota(jnp.int32, (8, BLK), 0)
        u, w = r[0], e[0]
        for i in range(1, 8):
            u = jnp.where(sub == i, r[i], u)
            w = jnp.where(sub == i, e[i], w)
        g_ref[rows, :] = u
        e_ref[rows, :] = w
        if p < 14:
            turned = jnp.transpose(u)
            for g in range(p + 2, 16):
                vg = [lanes(turned[8 * g : 8 * g + 8, :], i) for i in range(8)]
                there = pl.ds(8 * g, 8)
                g_ref[there, :] = g_ref[there, :] - sum_products(vg, r)
                e_ref[there, :] = e_ref[there, :] - sum_products(vg, e)


def halves(x):
    high = x.astype(BF16)
    return high, (x - high.astype(F32)).astype(BF16)


def dot3(a, b, ca, cb):
    return dot(a[0], b[0], ca, cb) + (dot(a[0], b[1], ca, cb) + dot(a[1], b[0], ca, cb))


def cholesky_kernel(
    a_ref, m_hbm, l_ref, s_ref, d_ref, g_ref, e_ref, nh_ref, nl_ref, m_ref, sem
):
    half = BLK // 2
    for r in range(KS):
        for c in range(r, KS):
            cols = slice(c * BLK, (c + 1) * BLK)
            lower = a_ref[r, KS] if c == r else a_ref[r, c]
            s_ref[r * BLK : r * BLK + half, cols] = a_ref[c, r].astype(F32)
            s_ref[r * BLK + half : (r + 1) * BLK, cols] = lower.astype(F32)
    row_id = lax.broadcasted_iota(jnp.int32, (BLK, BLK), 0)
    col_id = lax.broadcasted_iota(jnp.int32, (BLK, BLK), 1)
    ident = (row_id == col_id).astype(F32)

    @pl.loop(0, KS)
    def _(k):
        here = pl.ds(pl.multiple_of(k * BLK, BLK), BLK)
        g_ref[...] = s_ref[here, here]
        e_ref[...] = ident
        factor(g_ref, e_ref)
        d_ref[here, :] = g_ref[...]
        s_ref[here, here] = ident
        row = dot3(halves(e_ref[...]), halves(s_ref[here, :]), 1, 0)
        s_ref[here, :] = row
        nh_ref[...], nl_ref[...] = halves(row)
        keep = lax.broadcasted_iota(jnp.int32, (BLK, ORDER), 1) < (k + 1) * BLK
        m_ref[here, :] = jnp.where(keep, row, 0.0).astype(BF16)

        @pl.loop(k + 1, KS)
        def _(i):
            there = pl.ds(pl.multiple_of(i * BLK, BLK), BLK)
            s_ref[there, here] = jnp.zeros((BLK, BLK), F32)
            part = nh_ref[:, there], nl_ref[:, there]
            s_ref[there, :] = s_ref[there, :] - dot3(part, (nh_ref[...], nl_ref[...]), 0, 0)

    out = pltpu.make_async_copy(m_ref, m_hbm, sem)
    out.start()
    leaf, front = place()
    front = jnp.minimum(front, KS - 1)
    mine = pl.ds(pl.multiple_of(leaf * BLK, BLK), BLK)
    other = pl.ds(pl.multiple_of(front * BLK, BLK), BLK)
    upper = jnp.where(row_id <= col_id, d_ref[mine, :], 0.0)
    beyond = jnp.where(front < leaf, s_ref[other, mine], 0.0)
    l_ref[...] = jnp.transpose(jnp.where(front == leaf, upper, beyond))
    out.wait()


def cholesky(a):
    return pl.pallas_call(
        cholesky_kernel,
        name="cholesky",
        out_shape=(
            jax.ShapeDtypeStruct((ORDER, ORDER), BF16),
            jax.ShapeDtypeStruct((BLK, BLK), F32),
        ),
        in_specs=[WHOLE],
        out_specs=(pl.BlockSpec(memory_space=pltpu.HBM), WHOLE),
        scratch_shapes=[
            pltpu.VMEM((ORDER, ORDER), F32),
            pltpu.VMEM((ORDER, BLK), F32),
            pltpu.VMEM((BLK, BLK), F32),
            pltpu.VMEM((BLK, BLK), F32),
            pltpu.VMEM((BLK, ORDER), BF16),
            pltpu.VMEM((BLK, ORDER), BF16),
            pltpu.VMEM((ORDER, ORDER), BF16),
            pltpu.SemaphoreType.DMA,
        ],
        compiler_params=pltpu.CompilerParams(vmem_limit_bytes=24 << 20),
        cost_estimate=pl.CostEstimate(
            flops=60_000_000_000, bytes_accessed=6 << 20, transcendentals=1024
        ),
    )(a)


def schur_kernel(
    map_ref, l_ref, given_ref, upper_ref, panel_ref, m_hbm, cols_hbm, rows_hbm, front_ref,
    out_ref, m_ref, cols_ref, rows_ref, lower_ref, w_ref, low_ref, update_ref, sem
):
    step = pl.program_id(0)
    leaf, front = place()
    owner = jnp.minimum(front, KS - 1)
    rows_here = STEP_ROWS * BLK

    def copies():
        yield pltpu.make_async_copy(m_hbm, m_ref, sem.at[2, 0])
        yield pltpu.make_async_copy(cols_hbm, cols_ref, sem.at[2, 1])
        for b in range(2):
            for a in range(KS):
                columns = pl.ds(a * BLK, BLK)
                source = rows_hbm.at[b, a]
                yield pltpu.make_async_copy(
                    source.at[pl.ds(0, ORDER)], rows_ref.at[b, :, columns], sem.at[b, a]
                )
                yield pltpu.make_async_copy(
                    source.at[pl.ds(ORDER, 2 * BLK)], lower_ref.at[b, a], sem.at[3 + b, a]
                )

    @pl.when(step == 0)
    def _():
        for copy in copies():
            copy.start()
        for c in range(N_LEAF):
            update_ref[c, 0] = update_of(given_ref[c, 0], rows_of(upper_ref, c), panel_ref[c])
        waits = list(copies())
        waits[0].wait()
        waits[1].wait()
        for n in range(4):
            take = slice(n * 256, (n + 1) * 256)
            upto = slice(0, (n + 1) * 256)
            w_ref[take, :] = dot(m_ref[take, upto], cols_ref[upto, :], 1, 0).astype(BF16)
        for copy in waits[2:]:
            copy.wait()
        for c in range(N_LEAF):
            product = jnp.zeros((BLK, BLK), F32)
            for n in range(4):
                part = slice(n * BLK // 2, (n + 1) * BLK // 2)
                rows = jnp.concatenate([lower_ref[0, c, part], lower_ref[1, c, part]], axis=0)
                product += dot(rows, panel_ref[c, :, n * BLK : (n + 1) * BLK], 1, 1)
            update_ref[c, 1] = (given_ref[c, 1].astype(F32) - product).astype(BF16)

    for q in range(STEP_ROWS):
        source = pl.ds(pl.multiple_of((step * (STEP_ROWS // 2) + q // 2) * BLK, BLK), BLK)
        mine = slice(q * BLK, (q + 1) * BLK)
        for n in range(4):
            take = slice(n * 256, (n + 1) * 256)
            upto = slice(0, (n + 1) * 256)
            low_ref[mine, take] = dot(rows_ref[q % 2, source, upto], m_ref[take, upto], 1, 1)
    low = low_ref[...].astype(BF16)
    for n in range(4):
        part = dot(low, w_ref[:, n * 256 : (n + 1) * 256], 1, 0)
        for s in range(2):
            there = pl.ds(2 * n + s, rows_here, stride=8)
            out_ref[there, :] = front_ref[there, :] - part[:, s * BLK : (s + 1) * BLK]
    for c in range(N_LEAF):
        s = map_ref[c, front] // N_FRONT
        for b in range(2):
            q = map_ref[c, leaf + b * N_LEAF] // N_FRONT * 2 + b - step * STEP_ROWS

            @pl.when((q >= 0) & (q < STEP_ROWS))
            def _():
                there = pl.ds(q * (8 * BLK) + s, BLK, stride=8)
                out_ref[there, :] = out_ref[there, :] + update_ref[c, b].astype(F32)

    @pl.when(front < KS)
    def _():
        column = pl.ds(pl.multiple_of(owner * BLK, BLK), BLK)
        out_ref[pl.ds(0, rows_here, stride=8), :] = low_ref[:, column]

    @pl.when(step == 0)
    def _():
        out_ref[: 8 * BLK, :] = jnp.zeros((8 * BLK, BLK), F32)

        @pl.when(front < KS)
        def _():
            out_ref[pl.ds(0, BLK, stride=8), :] = l_ref[...]


def schur(child_map, low, given, upper, panels, m, cols, rows, front):
    steps = 16 // STEP_ROWS
    block = pl.BlockSpec((STEP_ROWS * BLK * 8, BLK), lambda i: (i, 0))
    return pl.pallas_call(
        schur_kernel,
        name="schur",
        grid=(steps,),
        out_shape=jax.ShapeDtypeStruct((16 * BLK * 8, BLK), F32),
        in_specs=[TABLE] + [WHOLE] * 4 + [pl.BlockSpec(memory_space=pltpu.HBM)] * 3 + [block],
        out_specs=block,
        scratch_shapes=[
            pltpu.VMEM((ORDER, ORDER), BF16),
            pltpu.VMEM((ORDER, ORDER), BF16),
            pltpu.VMEM((2, ORDER, ORDER), BF16),
            pltpu.VMEM((2, KS, 2 * BLK, BLK), BF16),
            pltpu.VMEM((ORDER, ORDER), BF16),
            pltpu.VMEM((STEP_ROWS * BLK, ORDER), F32),
            pltpu.VMEM((N_LEAF, 2, BLK, BLK), BF16),
            pltpu.SemaphoreType.DMA((5, KS)),
        ],
        compiler_params=pltpu.CompilerParams(vmem_limit_bytes=48 << 20),
    )(child_map, low, given, upper, panels, m, cols, rows, front)


def gather(x, axis, count):
    spread = jnp.broadcast_to(x[None], (count, *x.shape))
    return lax.all_to_all(spread, axis, 0, 0)


def exchange(flip):
    return [
        (a * N_FRONT + b * N_LEAF + c, c * N_FRONT + (b ^ flip) * N_LEAF + a)
        for a in range(N_LEAF)
        for b in range(2)
        for c in range(N_LEAF)
    ]


def one_pass(front_entries, child_panels, child_blocks, child_map):
    front = front_entries.reshape(16 * BLK * 8, BLK)
    front_id = lax.axis_index("front")
    leaf_id = lax.axis_index("leaf")
    own = child_panels[0]
    panels = lax.all_gather(own, "leaf", axis=0)
    halves_of = own.reshape(2, BLK // 2, own.shape[1])
    early = front_id < N_LEAF
    same = lax.ppermute(jnp.where(early, halves_of[0], halves_of[1]), MESH_AXES, exchange(0))
    other = lax.ppermute(jnp.where(early, halves_of[1], halves_of[0]), MESH_AXES, exchange(1))
    upper = gather(jnp.where(early, same, other), "front", N_FRONT)
    upper = upper.reshape(2, N_LEAF, BLK // 2, own.shape[1])
    lower = jnp.where(early, other, same).reshape(BLK // 2, 4, BLK).transpose(1, 0, 2)
    blocks = child_blocks[0].reshape(2, N_LEAF, BLK, BLK).transpose(1, 0, 2, 3)
    blocks, upper = lax.optimization_barrier((blocks, upper))
    given = lax.all_to_all(blocks, "leaf", 0, 0)
    flat, turned, first = pivot_rows(child_map, front, given, upper, panels)
    turned = lax.ppermute(turned, MESH_AXES, exchange(0))
    packed = jnp.concatenate([turned.reshape(ORDER, BLK), lower.reshape(2 * BLK, BLK)], axis=0)
    pieces = gather(first, "front", N_FRONT)[:KS]
    packed, pieces = lax.optimization_barrier((packed, pieces))
    rows = lax.all_gather(packed, "front", axis=0)
    extra = lax.dynamic_index_in_dim(pieces[:, 1], leaf_id, 0, keepdims=True)
    whole = jnp.concatenate([pieces[:, 0], extra], axis=0)
    separator = gather(whole, "leaf", N_LEAF)
    flat, separator = lax.optimization_barrier((flat, separator))
    cols = lax.all_gather(flat, "leaf", axis=0, tiled=True)
    m, low = cholesky(separator)
    rows = rows.reshape(2, KS, ORDER + 2 * BLK, BLK)
    out = schur(child_map, low, given, upper, panels, m, cols, rows, front)
    return out.reshape(16, 1, BLK, 8, 1, BLK)


def solution(mesh):
    placed = (
        P(None, "leaf", None, None, "front", None),
        P("leaf", "front", None),
        P("leaf", None, "front"),
        P(),
    )
    return jax.shard_map(
        one_pass,
        mesh=mesh,
        in_specs=placed,
        out_specs=P(None, "leaf", None, None, "front", None),
        check_vma=False,
    )
```

```python
import jax
import jax.numpy as jnp
from jax import lax
from jax.experimental import pallas as pl
from jax.experimental.pallas import tpu as pltpu
from jax.sharding import PartitionSpec as P


F32 = jnp.float32
BF16 = jnp.bfloat16
KS = 8
BLK = 128
ORDER = KS * BLK
N_LEAF = 8
N_FRONT = 16
STEP_ROWS = 4
MESH_AXES = ("leaf", "front")
WHOLE = pl.BlockSpec(memory_space=pltpu.VMEM)
TABLE = pl.BlockSpec(memory_space=pltpu.SMEM)


def dot(a, b, ca, cb, precision=None):
    return lax.dot_general(
        a, b, (((ca,), (cb,)), ((), ())), precision=precision, preferred_element_type=F32
    )


def place():
    return lax.axis_index("leaf"), lax.axis_index("front")


def rows_of(rows_ref, c):
    return jnp.concatenate([rows_ref[0, c], rows_ref[1, c]], axis=0)


def update_of(given, left, right):
    return (given.astype(F32) - dot(left, right, 1, 1)).astype(BF16)


def pivot_kernel(
    map_ref, front_ref, given_ref, rows_ref, cols_ref, flat_ref, turned_ref, first_ref, sum_ref
):
    leaf, front = place()
    for s in range(8):
        sum_ref[:, s * BLK : (s + 1) * BLK] = front_ref[pl.ds(s, BLK, stride=8), :]
    for c in range(N_LEAF):
        cycle = map_ref[c, front] // N_FRONT

        @pl.when(map_ref[c, leaf] // N_FRONT == 0)
        def _():
            cols = pl.ds(pl.multiple_of(cycle * BLK, BLK), BLK)
            update = update_of(given_ref[c, 0], rows_of(rows_ref, c), cols_ref[c])
            sum_ref[:, cols] += update.astype(F32)

    flat_ref[...] = sum_ref[...].astype(BF16)
    for s in range(8):
        turned_ref[s] = jnp.transpose(sum_ref[:, s * BLK : (s + 1) * BLK]).astype(BF16)
    half = BLK // 2
    bottom = sum_ref[half:, :BLK]
    top = jnp.where(leaf > front, jnp.transpose(sum_ref[:, :BLK])[:half], sum_ref[:half, :BLK])
    first_ref[0] = jnp.where(leaf < front, bottom, top).astype(BF16)
    first_ref[1] = bottom.astype(BF16)


def pivot_rows(child_map, front, given, rows, cols):
    return pl.pallas_call(
        pivot_kernel,
        name="pivot_rows",
        grid=(1,),
        out_shape=(
            jax.ShapeDtypeStruct((BLK, 8 * BLK), BF16),
            jax.ShapeDtypeStruct((8, BLK, BLK), BF16),
            jax.ShapeDtypeStruct((2, BLK // 2, BLK), BF16),
        ),
        in_specs=[
            TABLE,
            pl.BlockSpec((8 * BLK, BLK), lambda i: (0, 0)),
            pl.BlockSpec((N_LEAF, 1, BLK, BLK), lambda i: (0, 0, 0, 0)),
            pl.BlockSpec(rows.shape, lambda i: (0, 0, 0, 0)),
            pl.BlockSpec(cols.shape, lambda i: (0, 0, 0)),
        ],
        out_specs=(
            pl.BlockSpec((BLK, 8 * BLK), lambda i: (0, 0)),
            pl.BlockSpec((8, BLK, BLK), lambda i: (0, 0, 0)),
            pl.BlockSpec((2, BLK // 2, BLK), lambda i: (0, 0, 0)),
        ),
        scratch_shapes=[pltpu.VMEM((BLK, 8 * BLK), F32)],
    )(child_map, front, given, rows, cols)


def lanes(x, j):
    return jnp.broadcast_to(x[:, j : j + 1], (8, BLK))


def spread(ref, i):
    return ref[pl.ds(i, 8, stride=0), :]


def sum_products(v, r):
    t = [v[i] * r[i] for i in range(8)]
    while len(t) > 1:
        t = [t[i] + t[i + 1] for i in range(0, len(t), 2)]
    return t[0]


def high_part(x):
    return x.astype(BF16).astype(F32)


def factor(g_ref, e_ref, c_ref):
    for p in range(16):
        rows = pl.ds(8 * p, 8)
        below = pl.ds(8 * p + 8, 8)
        top = g_ref[rows, :]
        slot = p % 2 * 64
        for j in range(8):
            c_ref[slot + 8 * j : slot + 8 * j + 8, :] = lanes(top, 8 * p + j)
        a = [
            [spread(c_ref, slot + 8 * j + i) if j <= i else None for j in range(8)]
            for i in range(8)
        ]
        r = [spread(g_ref, 8 * p + i) for i in range(8)]
        e = [spread(e_ref, 8 * p + i) for i in range(8)]
        more = p < 15
        if more:
            after = g_ref[below, :]
            v = [lanes(after, 8 * p + j) for j in range(8)]
        for j in range(8):
            inv = lax.rsqrt(a[j][j])
            r[j] = r[j] * inv
            e[j] = e[j] * inv
            if more:
                v[j] = v[j] * inv
            col = [None] * 8
            for i in range(j + 1, 8):
                col[i] = a[i][j] * inv
            for i in range(j + 1, 8):
                for k in range(j + 1, i + 1):
                    a[i][k] = a[i][k] - col[i] * col[k]
            for i in range(j + 1, 8):
                r[i] = r[i] - col[i] * r[j]
                e[i] = e[i] - col[i] * e[j]
                if more:
                    v[i] = v[i] - col[i] * v[j]
        if more:
            g_ref[below, :] = after - sum_products(v, r)
            e_ref[below, :] = e_ref[below, :] - sum_products(v, e)
        sub = lax.broadcasted_iota(jnp.int32, (8, BLK), 0)
        u, w = r[0], e[0]
        for i in range(1, 8):
            u = jnp.where(sub == i, r[i], u)
            w = jnp.where(sub == i, e[i], w)
        g_ref[rows, :] = u
        e_ref[rows, :] = w
        if p < 14:
            turned = jnp.transpose(u)[8 * p + 16 : 8 * p + 24, :]
            vg = [lanes(turned, i) for i in range(8)]
            there = pl.ds(8 * p + 16, 8)
            g_ref[there, :] = g_ref[there, :] - sum_products(vg, r)
            e_ref[there, :] = e_ref[there, :] - sum_products(vg, e)
        if p < 13:
            uh, wh = high_part(u), high_part(w)
            ul, wl = u - uh, w - wh
            left = jnp.concatenate([uh, uh, ul, ul], axis=0).astype(BF16)
            top = jnp.concatenate([uh, wh], axis=1)
            low = jnp.concatenate([ul, wl], axis=1)
            right = jnp.concatenate([top, low, top, low], axis=0).astype(BF16)
            both = dot(left, right, 0, 0)
            there = slice(8 * p + 24, BLK)
            g_ref[there, :] = g_ref[there, :] - both[there, :BLK]
            e_ref[there, :] = e_ref[there, :] - both[there, BLK:]


def halves(x):
    high = x.astype(BF16)
    return high, (x - high.astype(F32)).astype(BF16)


def cholesky_kernel(
    *refs
):
    piece_refs, refs = refs[:N_LEAF], refs[N_LEAF:]
    (m_hbm, l_ref, s_ref, d_ref, g_ref, e_ref, nl_ref, nr_ref, m_ref, c_ref, sem) = refs
    leaf, front = place()
    half = BLK // 2
    for k in range(N_LEAF):
        giver = (leaf + N_LEAF - k) % N_LEAF * BLK
        for j in range(KS + 1):
            top = j * BLK <= giver
            row = jnp.where(top, j * BLK, giver + half) if j < KS else giver + half
            col = jnp.where(top, giver, j * BLK) if j < KS else giver
            rows = pl.ds(pl.multiple_of(row, half), half)
            s_ref[rows, pl.ds(pl.multiple_of(col, BLK), BLK)] = piece_refs[k][j].astype(F32)
    row_id = lax.broadcasted_iota(jnp.int32, (BLK, BLK), 0)
    col_id = lax.broadcasted_iota(jnp.int32, (BLK, BLK), 1)
    ident = (row_id == col_id).astype(F32)

    @pl.loop(0, KS)
    def _(k):
        here = pl.ds(pl.multiple_of(k * BLK, BLK), BLK)
        g_ref[...] = s_ref[here, here]
        e_ref[...] = ident
        factor(g_ref, e_ref, c_ref)
        d_ref[here, :] = g_ref[...]
        s_ref[here, here] = ident
        eh, el = halves(e_ref[...])
        sh, sl = halves(s_ref[here, :])
        left = jnp.concatenate([eh, el, eh], axis=1)
        row = dot(left, jnp.concatenate([sh, sh, sl], axis=0), 1, 0)
        s_ref[here, :] = row
        high, low = halves(row)
        for n in range(3):
            part = slice(n * BLK, (n + 1) * BLK)
            nl_ref[part, :] = low if n == 1 else high
            nr_ref[part, :] = low if n == 2 else high
        keep = lax.broadcasted_iota(jnp.int32, (BLK, ORDER), 1) < (k + 1) * BLK
        m_ref[here, :] = jnp.where(keep, row, 0.0).astype(BF16)

        @pl.loop(k + 1, KS)
        def _(i):
            there = pl.ds(pl.multiple_of(i * BLK, BLK), BLK)
            s_ref[there, here] = jnp.zeros((BLK, BLK), F32)
            s_ref[there, :] = s_ref[there, :] - dot(nl_ref[:, there], nr_ref[...], 0, 0)

    out = pltpu.make_async_copy(m_ref, m_hbm, sem)
    out.start()
    front = jnp.minimum(front, KS - 1)
    mine = pl.ds(pl.multiple_of(leaf * BLK, BLK), BLK)
    other = pl.ds(pl.multiple_of(front * BLK, BLK), BLK)
    upper = jnp.where(row_id <= col_id, d_ref[mine, :], 0.0)
    beyond = jnp.where(front < leaf, s_ref[other, mine], 0.0)
    l_ref[...] = jnp.transpose(jnp.where(front == leaf, upper, beyond))
    out.wait()


def cholesky(pieces):
    return pl.pallas_call(
        cholesky_kernel,
        name="cholesky",
        out_shape=(
            jax.ShapeDtypeStruct((ORDER, ORDER), BF16),
            jax.ShapeDtypeStruct((BLK, BLK), F32),
        ),
        in_specs=[WHOLE] * N_LEAF,
        out_specs=(pl.BlockSpec(memory_space=pltpu.HBM), WHOLE),
        scratch_shapes=[
            pltpu.VMEM((ORDER, ORDER), F32),
            pltpu.VMEM((ORDER, BLK), F32),
            pltpu.VMEM((BLK, BLK), F32),
            pltpu.VMEM((BLK, BLK), F32),
            pltpu.VMEM((3 * BLK, ORDER), BF16),
            pltpu.VMEM((3 * BLK, ORDER), BF16),
            pltpu.VMEM((ORDER, ORDER), BF16),
            pltpu.VMEM((BLK, BLK), F32),
            pltpu.SemaphoreType.DMA,
        ],
        compiler_params=pltpu.CompilerParams(vmem_limit_bytes=24 << 20),
        cost_estimate=pl.CostEstimate(
            flops=60_000_000_000, bytes_accessed=6 << 20, transcendentals=1024
        ),
    )(*pieces)


def schur_kernel(
    map_ref, l_ref, given_ref, upper_ref, panel_ref, m_hbm, cols_hbm, rows_hbm, front_ref,
    out_ref, m_ref, cols_ref, rows_ref, lower_ref, w_ref, low_ref, update_ref, sem
):
    step = pl.program_id(0)
    leaf, front = place()
    owner = jnp.minimum(front, KS - 1)

    def copies():
        yield pltpu.make_async_copy(m_hbm, m_ref, sem.at[2, 0])
        yield pltpu.make_async_copy(cols_hbm, cols_ref, sem.at[2, 1])
        for b in range(2):
            for a in range(KS):
                columns = pl.ds(a * BLK, BLK)
                source = rows_hbm.at[b, a]
                yield pltpu.make_async_copy(
                    source.at[pl.ds(0, ORDER)], rows_ref.at[b, :, columns], sem.at[b, a]
                )
                yield pltpu.make_async_copy(
                    source.at[pl.ds(ORDER, 2 * BLK)], lower_ref.at[b, a], sem.at[3 + b, a]
                )

    @pl.when(step == 0)
    def _():
        for copy in copies():
            copy.start()
        for c in range(N_LEAF):
            update_ref[c, 0] = update_of(given_ref[c, 0], rows_of(upper_ref, c), panel_ref[c])
        waits = list(copies())
        waits[0].wait()
        waits[1].wait()
        for n in range(4):
            take = slice(n * 256, (n + 1) * 256)
            upto = slice(0, (n + 1) * 256)
            w_ref[take, :] = dot(m_ref[take, upto], cols_ref[upto, :], 1, 0).astype(BF16)
        for copy in waits[2:]:
            copy.wait()
        for c in range(N_LEAF):
            product = jnp.zeros((BLK, BLK), F32)
            for n in range(4):
                part = slice(n * BLK // 2, (n + 1) * BLK // 2)
                rows = jnp.concatenate([lower_ref[0, c, part], lower_ref[1, c, part]], axis=0)
                product += dot(rows, panel_ref[c, :, n * BLK : (n + 1) * BLK], 1, 1)
            update_ref[c, 1] = (given_ref[c, 1].astype(F32) - product).astype(BF16)

    pair = STEP_ROWS // 2 * BLK
    source = pl.ds(pl.multiple_of(step * pair, pair), pair)
    for n in range(4):
        take = slice(n * 256, (n + 1) * 256)
        upto = slice(0, (n + 1) * 256)
        both = jnp.concatenate([rows_ref[0, source, upto], rows_ref[1, source, upto]], axis=0)
        low_ref[:, take] = dot(both, m_ref[take, upto], 1, 1)
    low = low_ref[...].astype(BF16)
    order = [q % 2 * pair + q // 2 * BLK for q in range(STEP_ROWS)]
    for n in range(4):
        part = dot(low, w_ref[:, n * 256 : (n + 1) * 256], 1, 0)
        for s in range(2):
            for q, at in enumerate(order):
                there = pl.ds(q * 8 * BLK + 2 * n + s, BLK, stride=8)
                product = part[at : at + BLK, s * BLK : (s + 1) * BLK]
                out_ref[there, :] = front_ref[there, :] - product
    for c in range(N_LEAF):
        s = map_ref[c, front] // N_FRONT
        for b in range(2):
            q = map_ref[c, leaf + b * N_LEAF] // N_FRONT * 2 + b - step * STEP_ROWS

            @pl.when((q >= 0) & (q < STEP_ROWS))
            def _():
                there = pl.ds(q * (8 * BLK) + s, BLK, stride=8)
                out_ref[there, :] = out_ref[there, :] + update_ref[c, b].astype(F32)

    @pl.when(front < KS)
    def _():
        column = pl.ds(pl.multiple_of(owner * BLK, BLK), BLK)
        for q, at in enumerate(order):
            out_ref[pl.ds(q * 8 * BLK, BLK, stride=8), :] = low_ref[at : at + BLK, column]

    @pl.when(step == 0)
    def _():
        out_ref[: 8 * BLK, :] = jnp.zeros((8 * BLK, BLK), F32)

        @pl.when(front < KS)
        def _():
            out_ref[pl.ds(0, BLK, stride=8), :] = l_ref[...]


def schur(child_map, low, given, upper, panels, m, cols, rows, front):
    steps = 16 // STEP_ROWS
    block = pl.BlockSpec((STEP_ROWS * BLK * 8, BLK), lambda i: (i, 0))
    return pl.pallas_call(
        schur_kernel,
        name="schur",
        grid=(steps,),
        out_shape=jax.ShapeDtypeStruct((16 * BLK * 8, BLK), F32),
        in_specs=[TABLE] + [WHOLE] * 4 + [pl.BlockSpec(memory_space=pltpu.HBM)] * 3 + [block],
        out_specs=block,
        scratch_shapes=[
            pltpu.VMEM((ORDER, ORDER), BF16),
            pltpu.VMEM((ORDER, ORDER), BF16),
            pltpu.VMEM((2, ORDER, ORDER), BF16),
            pltpu.VMEM((2, KS, 2 * BLK, BLK), BF16),
            pltpu.VMEM((ORDER, ORDER), BF16),
            pltpu.VMEM((STEP_ROWS * BLK, ORDER), F32),
            pltpu.VMEM((N_LEAF, 2, BLK, BLK), BF16),
            pltpu.SemaphoreType.DMA((5, KS)),
        ],
        compiler_params=pltpu.CompilerParams(vmem_limit_bytes=48 << 20),
    )(child_map, low, given, upper, panels, m, cols, rows, front)


def gather(x, axis, count):
    spread = jnp.broadcast_to(x[None], (count, *x.shape))
    return lax.all_to_all(spread, axis, 0, 0)


def exchange(flip):
    return [
        (a * N_FRONT + b * N_LEAF + c, c * N_FRONT + (b ^ flip) * N_LEAF + a)
        for a in range(N_LEAF)
        for b in range(2)
        for c in range(N_LEAF)
    ]


def one_pass(front_entries, child_panels, child_blocks, child_map):
    front = front_entries.reshape(16 * BLK * 8, BLK)
    front_id = lax.axis_index("front")
    leaf_id = lax.axis_index("leaf")
    own = child_panels[0]
    halves_of = own.reshape(2, BLK // 2, own.shape[1])
    early = front_id < N_LEAF
    same = lax.ppermute(jnp.where(early, halves_of[0], halves_of[1]), MESH_AXES, exchange(0))
    other = lax.ppermute(jnp.where(early, halves_of[1], halves_of[0]), MESH_AXES, exchange(1))
    blocks = child_blocks[0].reshape(2, N_LEAF, BLK, BLK).transpose(1, 0, 2, 3)
    given = lax.all_to_all(blocks, "leaf", 0, 0)
    own, same, other, given = lax.optimization_barrier((own, same, other, given))
    panels = lax.all_gather(own, "leaf", axis=0)
    upper = gather(jnp.where(early, same, other), "front", N_FRONT)
    upper = upper.reshape(2, N_LEAF, BLK // 2, own.shape[1])
    lower = jnp.where(early, other, same).reshape(BLK // 2, 4, BLK).transpose(1, 0, 2)
    flat, turned, first = pivot_rows(child_map, front, given, upper, panels)
    turned = lax.ppermute(turned, MESH_AXES, exchange(0))
    packed = jnp.concatenate([turned.reshape(ORDER, BLK), lower.reshape(2 * BLK, BLK)], axis=0)
    pieces = gather(first, "front", N_FRONT)[:KS]
    packed, pieces = lax.optimization_barrier((packed, pieces))
    rows = lax.all_gather(packed, "front", axis=0)
    extra = lax.dynamic_index_in_dim(pieces[:, 1], leaf_id, 0, keepdims=True)
    whole = jnp.concatenate([pieces[:, 0], extra], axis=0)
    separator = [whole] + [
        lax.ppermute(whole, "leaf", [(i, (i + k) % N_LEAF) for i in range(N_LEAF)])
        for k in range(1, N_LEAF)
    ]
    cols = lax.all_gather(flat, "leaf", axis=0, tiled=True)
    m, low = cholesky(separator)
    rows = rows.reshape(2, KS, ORDER + 2 * BLK, BLK)
    out = schur(child_map, low, given, upper, panels, m, cols, rows, front)
    return out.reshape(16, 1, BLK, 8, 1, BLK)


def solution(mesh):
    placed = (
        P(None, "leaf", None, None, "front", None),
        P("leaf", "front", None),
        P("leaf", None, "front"),
        P(),
    )
    return jax.shard_map(
        one_pass,
        mesh=mesh,
        in_specs=placed,
        out_specs=P(None, "leaf", None, None, "front", None),
        check_vma=False,
    )
```

```python
import jax
import jax.numpy as jnp
from jax import lax
from jax.experimental import pallas as pl
from jax.experimental.pallas import tpu as pltpu
from jax.sharding import PartitionSpec as P


F32 = jnp.float32
BF16 = jnp.bfloat16
KS = 8
BLK = 128
ORDER = KS * BLK
N_LEAF = 8
N_FRONT = 16
STEP_ROWS = 4
MESH_AXES = ("leaf", "front")
WHOLE = pl.BlockSpec(memory_space=pltpu.VMEM)
TABLE = pl.BlockSpec(memory_space=pltpu.SMEM)


def dot(a, b, ca, cb, precision=None):
    return lax.dot_general(
        a, b, (((ca,), (cb,)), ((), ())), precision=precision, preferred_element_type=F32
    )


def place():
    return lax.axis_index("leaf"), lax.axis_index("front")


def rows_of(rows_ref, c):
    return jnp.concatenate([rows_ref[0, c], rows_ref[1, c]], axis=0)


def update_of(given, left, right):
    return (given.astype(F32) - dot(left, right, 1, 1)).astype(BF16)


def pivot_kernel(
    map_ref, front_ref, given_ref, rows_ref, cols_ref, flat_ref, turned_ref, first_ref, sum_ref
):
    leaf, front = place()
    for s in range(8):
        sum_ref[:, s * BLK : (s + 1) * BLK] = front_ref[pl.ds(s, BLK, stride=8), :]
    for c in range(N_LEAF):
        cycle = map_ref[c, front] // N_FRONT

        @pl.when(map_ref[c, leaf] // N_FRONT == 0)
        def _():
            cols = pl.ds(pl.multiple_of(cycle * BLK, BLK), BLK)
            update = update_of(given_ref[c, 0], rows_of(rows_ref, c), cols_ref[c])
            sum_ref[:, cols] += update.astype(F32)

    flat_ref[...] = sum_ref[...].astype(BF16)
    for s in range(8):
        turned_ref[s] = jnp.transpose(sum_ref[:, s * BLK : (s + 1) * BLK]).astype(BF16)
    half = BLK // 2
    bottom = sum_ref[half:, :BLK]
    top = jnp.where(leaf > front, jnp.transpose(sum_ref[:, :BLK])[:half], sum_ref[:half, :BLK])
    first_ref[0] = jnp.where(leaf < front, bottom, top).astype(BF16)
    first_ref[1] = bottom.astype(BF16)


def pivot_rows(child_map, front, given, rows, cols):
    return pl.pallas_call(
        pivot_kernel,
        name="pivot_rows",
        grid=(1,),
        out_shape=(
            jax.ShapeDtypeStruct((BLK, 8 * BLK), BF16),
            jax.ShapeDtypeStruct((8, BLK, BLK), BF16),
            jax.ShapeDtypeStruct((2, BLK // 2, BLK), BF16),
        ),
        in_specs=[
            TABLE,
            pl.BlockSpec((8 * BLK, BLK), lambda i: (0, 0)),
            pl.BlockSpec((N_LEAF, 1, BLK, BLK), lambda i: (0, 0, 0, 0)),
            pl.BlockSpec(rows.shape, lambda i: (0, 0, 0, 0)),
            pl.BlockSpec(cols.shape, lambda i: (0, 0, 0)),
        ],
        out_specs=(
            pl.BlockSpec((BLK, 8 * BLK), lambda i: (0, 0)),
            pl.BlockSpec((8, BLK, BLK), lambda i: (0, 0, 0)),
            pl.BlockSpec((2, BLK // 2, BLK), lambda i: (0, 0, 0)),
        ),
        scratch_shapes=[pltpu.VMEM((BLK, 8 * BLK), F32)],
    )(child_map, front, given, rows, cols)


def lanes(x, j):
    return jnp.broadcast_to(x[:, j : j + 1], (8, BLK))


def spread(ref, i):
    return ref[pl.ds(i, 8, stride=0), :]


def sum_products(v, r):
    t = [v[i] * r[i] for i in range(8)]
    while len(t) > 1:
        t = [t[i] + t[i + 1] for i in range(0, len(t), 2)]
    return t[0]


def high_part(x):
    return x.astype(BF16).astype(F32)


def factor(g_ref, e_ref, c_ref):
    for p in range(16):
        rows = pl.ds(8 * p, 8)
        below = pl.ds(8 * p + 8, 8)
        top = g_ref[rows, :]
        slot = p % 2 * 64
        for j in range(8):
            c_ref[slot + 8 * j : slot + 8 * j + 8, :] = lanes(top, 8 * p + j)
        a = [
            [spread(c_ref, slot + 8 * j + i) if j <= i else None for j in range(8)]
            for i in range(8)
        ]
        r = [spread(g_ref, 8 * p + i) for i in range(8)]
        e = [spread(e_ref, 8 * p + i) for i in range(8)]
        more = p < 15
        if more:
            after = g_ref[below, :]
            v = [lanes(after, 8 * p + j) for j in range(8)]
        for j in range(8):
            inv = lax.rsqrt(a[j][j])
            r[j] = r[j] * inv
            e[j] = e[j] * inv
            if more:
                v[j] = v[j] * inv
            col = [None] * 8
            for i in range(j + 1, 8):
                col[i] = a[i][j] * inv
            for i in range(j + 1, 8):
                for k in range(j + 1, i + 1):
                    a[i][k] = a[i][k] - col[i] * col[k]
            for i in range(j + 1, 8):
                r[i] = r[i] - col[i] * r[j]
                e[i] = e[i] - col[i] * e[j]
                if more:
                    v[i] = v[i] - col[i] * v[j]
        if more:
            g_ref[below, :] = after - sum_products(v, r)
            e_ref[below, :] = e_ref[below, :] - sum_products(v, e)
        sub = lax.broadcasted_iota(jnp.int32, (8, BLK), 0)
        u, w = r[0], e[0]
        for i in range(1, 8):
            u = jnp.where(sub == i, r[i], u)
            w = jnp.where(sub == i, e[i], w)
        g_ref[rows, :] = u
        e_ref[rows, :] = w
        if p < 14:
            turned = jnp.transpose(u)[8 * p + 16 : 8 * p + 24, :]
            vg = [lanes(turned, i) for i in range(8)]
            there = pl.ds(8 * p + 16, 8)
            g_ref[there, :] = g_ref[there, :] - sum_products(vg, r)
            e_ref[there, :] = e_ref[there, :] - sum_products(vg, e)
        if p < 13:
            uh, wh = high_part(u), high_part(w)
            ul, wl = u - uh, w - wh
            left = jnp.concatenate([uh, uh, ul, ul], axis=0).astype(BF16)
            top = jnp.concatenate([uh, wh], axis=1)
            low = jnp.concatenate([ul, wl], axis=1)
            right = jnp.concatenate([top, low, top, low], axis=0).astype(BF16)
            both = dot(left, right, 0, 0)
            there = slice(8 * p + 24, BLK)
            g_ref[there, :] = g_ref[there, :] - both[there, :BLK]
            e_ref[there, :] = e_ref[there, :] - both[there, BLK:]


def halves(x):
    high = x.astype(BF16)
    return high, (x - high.astype(F32)).astype(BF16)


def cholesky_kernel(
    *refs
):
    piece_refs, refs = refs[:N_LEAF], refs[N_LEAF:]
    (m_hbm, l_ref, s_ref, d_ref, g_ref, e_ref, nl_ref, nr_ref, m_ref, c_ref, sem) = refs
    leaf, front = place()
    half = BLK // 2
    for k in range(N_LEAF):
        giver = (leaf + N_LEAF - k) % N_LEAF * BLK
        for n in range(KS + 1):
            at = (n % 2 * 4 + (front + 4 - n // 2) % 4) * BLK
            top = at <= giver
            row = jnp.where(top, at, giver + half) if n < KS else giver + half
            col = jnp.where(top, giver, at) if n < KS else giver
            rows = pl.ds(pl.multiple_of(row, half), half)
            s_ref[rows, pl.ds(pl.multiple_of(col, BLK), BLK)] = piece_refs[k][n].astype(F32)
    row_id = lax.broadcasted_iota(jnp.int32, (BLK, BLK), 0)
    col_id = lax.broadcasted_iota(jnp.int32, (BLK, BLK), 1)
    ident = (row_id == col_id).astype(F32)

    @pl.loop(0, KS)
    def _(k):
        here = pl.ds(pl.multiple_of(k * BLK, BLK), BLK)
        g_ref[...] = s_ref[here, here]
        e_ref[...] = ident
        factor(g_ref, e_ref, c_ref)
        d_ref[here, :] = g_ref[...]
        s_ref[here, here] = ident
        eh, el = halves(e_ref[...])
        sh, sl = halves(s_ref[here, :])
        left = jnp.concatenate([eh, el, eh], axis=1)
        row = dot(left, jnp.concatenate([sh, sh, sl], axis=0), 1, 0)
        s_ref[here, :] = row
        high, low = halves(row)
        for n in range(3):
            part = slice(n * BLK, (n + 1) * BLK)
            nl_ref[part, :] = low if n == 1 else high
            nr_ref[part, :] = low if n == 2 else high
        keep = lax.broadcasted_iota(jnp.int32, (BLK, ORDER), 1) < (k + 1) * BLK
        m_ref[here, :] = jnp.where(keep, row, 0.0).astype(BF16)

        @pl.loop(k + 1, KS)
        def _(i):
            there = pl.ds(pl.multiple_of(i * BLK, BLK), BLK)
            s_ref[there, here] = jnp.zeros((BLK, BLK), F32)
            s_ref[there, :] = s_ref[there, :] - dot(nl_ref[:, there], nr_ref[...], 0, 0)

    out = pltpu.make_async_copy(m_ref, m_hbm, sem)
    out.start()
    front = jnp.minimum(front, KS - 1)
    mine = pl.ds(pl.multiple_of(leaf * BLK, BLK), BLK)
    other = pl.ds(pl.multiple_of(front * BLK, BLK), BLK)
    upper = jnp.where(row_id <= col_id, d_ref[mine, :], 0.0)
    beyond = jnp.where(front < leaf, s_ref[other, mine], 0.0)
    l_ref[...] = jnp.transpose(jnp.where(front == leaf, upper, beyond))
    out.wait()


def cholesky(pieces):
    return pl.pallas_call(
        cholesky_kernel,
        name="cholesky",
        out_shape=(
            jax.ShapeDtypeStruct((ORDER, ORDER), BF16),
            jax.ShapeDtypeStruct((BLK, BLK), F32),
        ),
        in_specs=[WHOLE] * N_LEAF,
        out_specs=(pl.BlockSpec(memory_space=pltpu.HBM), WHOLE),
        scratch_shapes=[
            pltpu.VMEM((ORDER, ORDER), F32),
            pltpu.VMEM((ORDER, BLK), F32),
            pltpu.VMEM((BLK, BLK), F32),
            pltpu.VMEM((BLK, BLK), F32),
            pltpu.VMEM((3 * BLK, ORDER), BF16),
            pltpu.VMEM((3 * BLK, ORDER), BF16),
            pltpu.VMEM((ORDER, ORDER), BF16),
            pltpu.VMEM((BLK, BLK), F32),
            pltpu.SemaphoreType.DMA,
        ],
        compiler_params=pltpu.CompilerParams(vmem_limit_bytes=52 << 20),
        cost_estimate=pl.CostEstimate(
            flops=60_000_000_000, bytes_accessed=6 << 20, transcendentals=1024
        ),
    )(*pieces)


def schur_kernel(
    map_ref, l_ref, given_ref, upper_ref, panel_ref, m_hbm, cols_hbm, rows_hbm, front_ref,
    out_ref, m_ref, cols_ref, rows_ref, lower_ref, w_ref, low_ref, update_ref, sem
):
    step = pl.program_id(0)
    leaf, front = place()
    owner = jnp.minimum(front, KS - 1)

    def copies():
        yield pltpu.make_async_copy(m_hbm, m_ref, sem.at[2, 0])
        yield pltpu.make_async_copy(cols_hbm, cols_ref, sem.at[2, 1])
        for b in range(2):
            for a in range(KS):
                columns = pl.ds(a * BLK, BLK)
                source = rows_hbm.at[b, a]
                yield pltpu.make_async_copy(
                    source.at[pl.ds(0, ORDER)], rows_ref.at[b, :, columns], sem.at[b, a]
                )
                yield pltpu.make_async_copy(
                    source.at[pl.ds(ORDER, 2 * BLK)], lower_ref.at[b, a], sem.at[3 + b, a]
                )

    @pl.when(step == 0)
    def _():
        for copy in copies():
            copy.start()
        for c in range(N_LEAF):
            update_ref[c, 0] = update_of(given_ref[c, 0], rows_of(upper_ref, c), panel_ref[c])
        waits = list(copies())
        waits[0].wait()
        waits[1].wait()
        for n in range(4):
            take = slice(n * 256, (n + 1) * 256)
            upto = slice(0, (n + 1) * 256)
            w_ref[take, :] = dot(m_ref[take, upto], cols_ref[upto, :], 1, 0).astype(BF16)
        for copy in waits[2:]:
            copy.wait()
        for c in range(N_LEAF):
            product = jnp.zeros((BLK, BLK), F32)
            for n in range(4):
                part = slice(n * BLK // 2, (n + 1) * BLK // 2)
                rows = jnp.concatenate([lower_ref[0, c, part], lower_ref[1, c, part]], axis=0)
                product += dot(rows, panel_ref[c, :, n * BLK : (n + 1) * BLK], 1, 1)
            update_ref[c, 1] = (given_ref[c, 1].astype(F32) - product).astype(BF16)

    pair = STEP_ROWS // 2 * BLK
    source = pl.ds(pl.multiple_of(step * pair, pair), pair)
    for n in range(4):
        take = slice(n * 256, (n + 1) * 256)
        upto = slice(0, (n + 1) * 256)
        both = jnp.concatenate([rows_ref[0, source, upto], rows_ref[1, source, upto]], axis=0)
        low_ref[:, take] = dot(both, m_ref[take, upto], 1, 1)
    low = low_ref[...].astype(BF16)
    order = [q % 2 * pair + q // 2 * BLK for q in range(STEP_ROWS)]
    for n in range(4):
        part = dot(low, w_ref[:, n * 256 : (n + 1) * 256], 1, 0)
        for s in range(2):
            for q, at in enumerate(order):
                there = pl.ds(q * 8 * BLK + 2 * n + s, BLK, stride=8)
                product = part[at : at + BLK, s * BLK : (s + 1) * BLK]
                out_ref[there, :] = front_ref[there, :] - product
    for c in range(N_LEAF):
        s = map_ref[c, front] // N_FRONT
        for b in range(2):
            q = map_ref[c, leaf + b * N_LEAF] // N_FRONT * 2 + b - step * STEP_ROWS

            @pl.when((q >= 0) & (q < STEP_ROWS))
            def _():
                there = pl.ds(q * (8 * BLK) + s, BLK, stride=8)
                out_ref[there, :] = out_ref[there, :] + update_ref[c, b].astype(F32)

    @pl.when(front < KS)
    def _():
        column = pl.ds(pl.multiple_of(owner * BLK, BLK), BLK)
        for q, at in enumerate(order):
            out_ref[pl.ds(q * 8 * BLK, BLK, stride=8), :] = low_ref[at : at + BLK, column]

    @pl.when(step == 0)
    def _():
        out_ref[: 8 * BLK, :] = jnp.zeros((8 * BLK, BLK), F32)

        @pl.when(front < KS)
        def _():
            out_ref[pl.ds(0, BLK, stride=8), :] = l_ref[...]


def schur(child_map, low, given, upper, panels, m, cols, rows, front):
    steps = 16 // STEP_ROWS
    block = pl.BlockSpec((STEP_ROWS * BLK * 8, BLK), lambda i: (i, 0))
    return pl.pallas_call(
        schur_kernel,
        name="schur",
        grid=(steps,),
        out_shape=jax.ShapeDtypeStruct((16 * BLK * 8, BLK), F32),
        in_specs=[TABLE] + [WHOLE] * 4 + [pl.BlockSpec(memory_space=pltpu.HBM)] * 3 + [block],
        out_specs=block,
        scratch_shapes=[
            pltpu.VMEM((ORDER, ORDER), BF16),
            pltpu.VMEM((ORDER, ORDER), BF16),
            pltpu.VMEM((2, ORDER, ORDER), BF16),
            pltpu.VMEM((2, KS, 2 * BLK, BLK), BF16),
            pltpu.VMEM((ORDER, ORDER), BF16),
            pltpu.VMEM((STEP_ROWS * BLK, ORDER), F32),
            pltpu.VMEM((N_LEAF, 2, BLK, BLK), BF16),
            pltpu.SemaphoreType.DMA((5, KS)),
        ],
        compiler_params=pltpu.CompilerParams(vmem_limit_bytes=52 << 20),
    )(child_map, low, given, upper, panels, m, cols, rows, front)


def gather(x, axis, count):
    spread = jnp.broadcast_to(x[None], (count, *x.shape))
    return lax.all_to_all(spread, axis, 0, 0)


def exchange(flip):
    return [
        (a * N_FRONT + b * N_LEAF + c, c * N_FRONT + (b ^ flip) * N_LEAF + a)
        for a in range(N_LEAF)
        for b in range(2)
        for c in range(N_LEAF)
    ]


def front_pieces(first, leaf_id, front_id):
    z, x = front_id // 4, front_id % 4
    got = [
        lax.ppermute(first, "front", [(4 * i + j, (i + k) % 4 * 4 + j) for i in (0, 1) for j in range(4)])
        for k in (1, 2, 3)
    ]
    near = jnp.where(z == 0, first, jnp.where(z == 1, got[0], jnp.where(z == 2, got[1], got[2])))
    far = jnp.where(z == 0, got[2], jnp.where(z == 1, first, jnp.where(z == 2, got[0], got[1])))
    extra = jnp.where(leaf_id < 4, near[1], far[1])
    mine = jnp.stack([near[0], far[0], extra])
    every = [mine] + [
        lax.ppermute(mine, "front", [(4 * i + j, 4 * i + (j + k) % 4) for i in range(4) for j in range(4)])
        for k in (1, 2, 3)
    ]
    at = (x + 8 - leaf_id) % 4
    extra = every[0][2]
    for k in (1, 2, 3):
        extra = jnp.where(at == k, every[k][2], extra)
    return jnp.concatenate([one[:2] for one in every] + [extra[None]], axis=0)


def one_pass(front_entries, child_panels, child_blocks, child_map):
    front = front_entries.reshape(16 * BLK * 8, BLK)
    front_id = lax.axis_index("front")
    leaf_id = lax.axis_index("leaf")
    own = child_panels[0]
    halves_of = own.reshape(2, BLK // 2, own.shape[1])
    early = front_id < N_LEAF
    same = lax.ppermute(jnp.where(early, halves_of[0], halves_of[1]), MESH_AXES, exchange(0))
    other = lax.ppermute(jnp.where(early, halves_of[1], halves_of[0]), MESH_AXES, exchange(1))
    blocks = child_blocks[0].reshape(2, N_LEAF, BLK, BLK).transpose(1, 0, 2, 3)
    given = lax.all_to_all(blocks, "leaf", 0, 0)
    own, same, other, given = lax.optimization_barrier((own, same, other, given))
    panels = lax.all_gather(own, "leaf", axis=0)
    upper = gather(jnp.where(early, same, other), "front", N_FRONT)
    upper = upper.reshape(2, N_LEAF, BLK // 2, own.shape[1])
    lower = jnp.where(early, other, same).reshape(BLK // 2, 4, BLK).transpose(1, 0, 2)
    flat, turned, first = pivot_rows(child_map, front, given, upper, panels)
    cols = lax.all_gather(flat, "leaf", axis=0, tiled=True)
    whole = front_pieces(first, leaf_id, front_id)
    separator = [whole] + [
        lax.ppermute(whole, "leaf", [(i, (i + k) % N_LEAF) for i in range(N_LEAF)])
        for k in range(1, N_LEAF)
    ]
    turned, whole = lax.optimization_barrier((turned, whole))
    turned = lax.ppermute(turned, MESH_AXES, exchange(0))
    packed = jnp.concatenate([turned.reshape(ORDER, BLK), lower.reshape(2 * BLK, BLK)], axis=0)
    rows = lax.all_gather(packed, "front", axis=0)
    m, low = cholesky(separator)
    rows = rows.reshape(2, KS, ORDER + 2 * BLK, BLK)
    out = schur(child_map, low, given, upper, panels, m, cols, rows, front)
    return out.reshape(16, 1, BLK, 8, 1, BLK)


def solution(mesh):
    placed = (
        P(None, "leaf", None, None, "front", None),
        P("leaf", "front", None),
        P("leaf", None, "front"),
        P(),
    )
    return jax.shard_map(
        one_pass,
        mesh=mesh,
        in_specs=placed,
        out_specs=P(None, "leaf", None, None, "front", None),
        check_vma=False,
    )
```

```python
import jax
import jax.numpy as jnp
from jax import lax
from jax.experimental import pallas as pl
from jax.experimental.pallas import tpu as pltpu
from jax.sharding import PartitionSpec as P


F32 = jnp.float32
BF16 = jnp.bfloat16
KS = 8
BLK = 128
ORDER = KS * BLK
N_LEAF = 8
N_FRONT = 16
STEP_ROWS = 4
MESH_AXES = ("leaf", "front")
WHOLE = pl.BlockSpec(memory_space=pltpu.VMEM)
TABLE = pl.BlockSpec(memory_space=pltpu.SMEM)


def dot(a, b, ca, cb, precision=None):
    return lax.dot_general(
        a, b, (((ca,), (cb,)), ((), ())), precision=precision, preferred_element_type=F32
    )


def place():
    return lax.axis_index("leaf"), lax.axis_index("front")


def rows_of(rows_ref, c):
    return jnp.concatenate([rows_ref[0, c], rows_ref[1, c]], axis=0)


def update_of(given, left, right):
    return (given.astype(F32) - dot(left, right, 1, 1)).astype(BF16)


def pivot_kernel(
    map_ref, front_ref, given_ref, rows_ref, cols_ref, flat_ref, turned_ref, first_ref, sum_ref
):
    leaf, front = place()
    for s in range(8):
        sum_ref[:, s * BLK : (s + 1) * BLK] = front_ref[pl.ds(s, BLK, stride=8), :]
    for c in range(N_LEAF):
        cycle = map_ref[c, front] // N_FRONT

        @pl.when(map_ref[c, leaf] // N_FRONT == 0)
        def _():
            cols = pl.ds(pl.multiple_of(cycle * BLK, BLK), BLK)
            update = update_of(given_ref[c, 0], rows_of(rows_ref, c), cols_ref[c])
            sum_ref[:, cols] += update.astype(F32)

    flat_ref[...] = sum_ref[...].astype(BF16)
    for s in range(8):
        turned_ref[s] = jnp.transpose(sum_ref[:, s * BLK : (s + 1) * BLK]).astype(BF16)
    half = BLK // 2
    bottom = sum_ref[half:, :BLK]
    top = jnp.where(leaf > front, jnp.transpose(sum_ref[:, :BLK])[:half], sum_ref[:half, :BLK])
    first_ref[0] = jnp.where(leaf < front, bottom, top).astype(BF16)
    first_ref[1] = bottom.astype(BF16)


def pivot_rows(child_map, front, given, rows, cols):
    return pl.pallas_call(
        pivot_kernel,
        name="pivot_rows",
        grid=(1,),
        out_shape=(
            jax.ShapeDtypeStruct((BLK, 8 * BLK), BF16),
            jax.ShapeDtypeStruct((8, BLK, BLK), BF16),
            jax.ShapeDtypeStruct((2, BLK // 2, BLK), BF16),
        ),
        in_specs=[
            TABLE,
            pl.BlockSpec((8 * BLK, BLK), lambda i: (0, 0)),
            pl.BlockSpec((N_LEAF, 1, BLK, BLK), lambda i: (0, 0, 0, 0)),
            pl.BlockSpec(rows.shape, lambda i: (0, 0, 0, 0)),
            pl.BlockSpec(cols.shape, lambda i: (0, 0, 0)),
        ],
        out_specs=(
            pl.BlockSpec((BLK, 8 * BLK), lambda i: (0, 0)),
            pl.BlockSpec((8, BLK, BLK), lambda i: (0, 0, 0)),
            pl.BlockSpec((2, BLK // 2, BLK), lambda i: (0, 0, 0)),
        ),
        scratch_shapes=[pltpu.VMEM((BLK, 8 * BLK), F32)],
    )(child_map, front, given, rows, cols)


def lanes(x, j):
    return jnp.broadcast_to(x[:, j : j + 1], (8, BLK))


def spread(ref, i):
    return ref[pl.ds(i, 8, stride=0), :]


def sum_products(v, r):
    t = [v[i] * r[i] for i in range(8)]
    while len(t) > 1:
        t = [t[i] + t[i + 1] for i in range(0, len(t), 2)]
    return t[0]


def high_part(x):
    return x.astype(BF16).astype(F32)


def factor(g_ref, e_ref, c_ref):
    for p in range(16):
        rows = pl.ds(8 * p, 8)
        below = pl.ds(8 * p + 8, 8)
        top = g_ref[rows, :]
        slot = p % 2 * 64
        for j in range(8):
            c_ref[slot + 8 * j : slot + 8 * j + 8, :] = lanes(top, 8 * p + j)
        a = [
            [spread(c_ref, slot + 8 * j + i) if j <= i else None for j in range(8)]
            for i in range(8)
        ]
        r = [spread(g_ref, 8 * p + i) for i in range(8)]
        e = [spread(e_ref, 8 * p + i) for i in range(8)]
        more = p < 15
        if more:
            after = g_ref[below, :]
            v = [lanes(after, 8 * p + j) for j in range(8)]
        for j in range(8):
            if j % 2 == 0:
                corner = a[j + 1][j + 1] * a[j][j] - a[j + 1][j] * a[j + 1][j]
                inv = lax.rsqrt(a[j][j])
                second = lax.rsqrt(corner) * (a[j][j] * inv)
            else:
                inv = second
            r[j] = r[j] * inv
            e[j] = e[j] * inv
            if more:
                v[j] = v[j] * inv
            col = [None] * 8
            for i in range(j + 1, 8):
                col[i] = a[i][j] * inv
            for i in range(j + 1, 8):
                for k in range(j + 1, i + 1):
                    if j % 2 or i > j + 1:
                        a[i][k] = a[i][k] - col[i] * col[k]
            for i in range(j + 1, 8):
                r[i] = r[i] - col[i] * r[j]
                e[i] = e[i] - col[i] * e[j]
                if more:
                    v[i] = v[i] - col[i] * v[j]
        if more:
            g_ref[below, :] = after - sum_products(v, r)
            e_ref[below, :] = e_ref[below, :] - sum_products(v, e)
        sub = lax.broadcasted_iota(jnp.int32, (8, BLK), 0)
        u, w = r[0], e[0]
        for i in range(1, 8):
            u = jnp.where(sub == i, r[i], u)
            w = jnp.where(sub == i, e[i], w)
        g_ref[rows, :] = u
        e_ref[rows, :] = w
        if p < 14:
            turned = jnp.transpose(u)[8 * p + 16 : 8 * p + 24, :]
            vg = [lanes(turned, i) for i in range(8)]
            there = pl.ds(8 * p + 16, 8)
            g_ref[there, :] = g_ref[there, :] - sum_products(vg, r)
            e_ref[there, :] = e_ref[there, :] - sum_products(vg, e)
        if p < 13:
            uh, wh = high_part(u), high_part(w)
            ul, wl = u - uh, w - wh
            left = jnp.concatenate([uh, uh, ul, ul], axis=0).astype(BF16)
            top = jnp.concatenate([uh, wh], axis=1)
            low = jnp.concatenate([ul, wl], axis=1)
            right = jnp.concatenate([top, low, top, low], axis=0).astype(BF16)
            both = dot(left, right, 0, 0)
            there = slice(8 * p + 24, BLK)
            g_ref[there, :] = g_ref[there, :] - both[there, :BLK]
            e_ref[there, :] = e_ref[there, :] - both[there, BLK:]


def halves(x):
    high = x.astype(BF16)
    return high, (x - high.astype(F32)).astype(BF16)


def cholesky_kernel(
    *refs
):
    piece_refs, refs = refs[:N_LEAF], refs[N_LEAF:]
    (m_hbm, l_ref, s_ref, d_ref, g_ref, e_ref, nl_ref, nr_ref, m_ref, c_ref, sem) = refs
    leaf, front = place()
    half = BLK // 2
    for k in range(N_LEAF):
        giver = (leaf + N_LEAF - k) % N_LEAF * BLK
        for n in range(KS + 1):
            at = (n % 2 * 4 + (front + 4 - n // 2) % 4) * BLK
            top = at <= giver
            row = jnp.where(top, at, giver + half) if n < KS else giver + half
            col = jnp.where(top, giver, at) if n < KS else giver
            rows = pl.ds(pl.multiple_of(row, half), half)
            s_ref[rows, pl.ds(pl.multiple_of(col, BLK), BLK)] = piece_refs[k][n].astype(F32)
    row_id = lax.broadcasted_iota(jnp.int32, (BLK, BLK), 0)
    col_id = lax.broadcasted_iota(jnp.int32, (BLK, BLK), 1)
    ident = (row_id == col_id).astype(F32)

    @pl.loop(0, KS)
    def _(k):
        here = pl.ds(pl.multiple_of(k * BLK, BLK), BLK)
        g_ref[...] = s_ref[here, here]
        e_ref[...] = ident
        factor(g_ref, e_ref, c_ref)
        d_ref[here, :] = g_ref[...]
        s_ref[here, here] = ident
        eh, el = halves(e_ref[...])
        sh, sl = halves(s_ref[here, :])
        left = jnp.concatenate([eh, el, eh], axis=1)
        row = dot(left, jnp.concatenate([sh, sh, sl], axis=0), 1, 0)
        s_ref[here, :] = row
        high, low = halves(row)
        for n in range(3):
            part = slice(n * BLK, (n + 1) * BLK)
            nl_ref[part, :] = low if n == 1 else high
            nr_ref[part, :] = low if n == 2 else high
        keep = lax.broadcasted_iota(jnp.int32, (BLK, ORDER), 1) < (k + 1) * BLK
        m_ref[here, :] = jnp.where(keep, row, 0.0).astype(BF16)

        @pl.loop(k + 1, KS)
        def _(i):
            there = pl.ds(pl.multiple_of(i * BLK, BLK), BLK)
            s_ref[there, here] = jnp.zeros((BLK, BLK), F32)
            s_ref[there, :] = s_ref[there, :] - dot(nl_ref[:, there], nr_ref[...], 0, 0)

    out = pltpu.make_async_copy(m_ref, m_hbm, sem)
    out.start()
    front = jnp.minimum(front, KS - 1)
    mine = pl.ds(pl.multiple_of(leaf * BLK, BLK), BLK)
    other = pl.ds(pl.multiple_of(front * BLK, BLK), BLK)
    upper = jnp.where(row_id <= col_id, d_ref[mine, :], 0.0)
    beyond = jnp.where(front < leaf, s_ref[other, mine], 0.0)
    l_ref[...] = jnp.transpose(jnp.where(front == leaf, upper, beyond))
    out.wait()


def cholesky(pieces):
    return pl.pallas_call(
        cholesky_kernel,
        name="cholesky",
        out_shape=(
            jax.ShapeDtypeStruct((ORDER, ORDER), BF16),
            jax.ShapeDtypeStruct((BLK, BLK), F32),
        ),
        in_specs=[WHOLE] * N_LEAF,
        out_specs=(pl.BlockSpec(memory_space=pltpu.HBM), WHOLE),
        scratch_shapes=[
            pltpu.VMEM((ORDER, ORDER), F32),
            pltpu.VMEM((ORDER, BLK), F32),
            pltpu.VMEM((BLK, BLK), F32),
            pltpu.VMEM((BLK, BLK), F32),
            pltpu.VMEM((3 * BLK, ORDER), BF16),
            pltpu.VMEM((3 * BLK, ORDER), BF16),
            pltpu.VMEM((ORDER, ORDER), BF16),
            pltpu.VMEM((BLK, BLK), F32),
            pltpu.SemaphoreType.DMA,
        ],
        compiler_params=pltpu.CompilerParams(vmem_limit_bytes=52 << 20),
        cost_estimate=pl.CostEstimate(
            flops=60_000_000_000, bytes_accessed=6 << 20, transcendentals=1024
        ),
    )(*pieces)


def schur_kernel(
    map_ref, l_ref, given_ref, upper_ref, panel_ref, m_hbm, cols_hbm, rows_hbm, front_ref,
    out_ref, m_ref, cols_ref, rows_ref, lower_ref, w_ref, low_ref, update_ref, sem
):
    step = pl.program_id(0)
    leaf, front = place()
    owner = jnp.minimum(front, KS - 1)

    def copies():
        yield pltpu.make_async_copy(m_hbm, m_ref, sem.at[2, 0])
        yield pltpu.make_async_copy(cols_hbm, cols_ref, sem.at[2, 1])
        for b in range(2):
            for a in range(KS):
                columns = pl.ds(a * BLK, BLK)
                source = rows_hbm.at[b, a]
                yield pltpu.make_async_copy(
                    source.at[pl.ds(0, ORDER)], rows_ref.at[b, :, columns], sem.at[b, a]
                )
                yield pltpu.make_async_copy(
                    source.at[pl.ds(ORDER, 2 * BLK)], lower_ref.at[b, a], sem.at[3 + b, a]
                )

    @pl.when(step == 0)
    def _():
        for copy in copies():
            copy.start()
        for c in range(N_LEAF):
            update_ref[c, 0] = update_of(given_ref[c, 0], rows_of(upper_ref, c), panel_ref[c])
        waits = list(copies())
        waits[0].wait()
        waits[1].wait()
        for n in range(4):
            take = slice(n * 256, (n + 1) * 256)
            upto = slice(0, (n + 1) * 256)
            w_ref[take, :] = dot(m_ref[take, upto], cols_ref[upto, :], 1, 0).astype(BF16)
        for copy in waits[2:]:
            copy.wait()
        for c in range(N_LEAF):
            product = jnp.zeros((BLK, BLK), F32)
            for n in range(4):
                part = slice(n * BLK // 2, (n + 1) * BLK // 2)
                rows = jnp.concatenate([lower_ref[0, c, part], lower_ref[1, c, part]], axis=0)
                product += dot(rows, panel_ref[c, :, n * BLK : (n + 1) * BLK], 1, 1)
            update_ref[c, 1] = (given_ref[c, 1].astype(F32) - product).astype(BF16)

    pair = STEP_ROWS // 2 * BLK
    source = pl.ds(pl.multiple_of(step * pair, pair), pair)
    for n in range(4):
        take = slice(n * 256, (n + 1) * 256)
        upto = slice(0, (n + 1) * 256)
        both = jnp.concatenate([rows_ref[0, source, upto], rows_ref[1, source, upto]], axis=0)
        low_ref[:, take] = dot(both, m_ref[take, upto], 1, 1)
    low = low_ref[...].astype(BF16)
    order = [q % 2 * pair + q // 2 * BLK for q in range(STEP_ROWS)]
    for n in range(4):
        part = dot(low, w_ref[:, n * 256 : (n + 1) * 256], 1, 0)
        for s in range(2):
            for q, at in enumerate(order):
                there = pl.ds(q * 8 * BLK + 2 * n + s, BLK, stride=8)
                product = part[at : at + BLK, s * BLK : (s + 1) * BLK]
                out_ref[there, :] = front_ref[there, :] - product
    for c in range(N_LEAF):
        s = map_ref[c, front] // N_FRONT
        for b in range(2):
            q = map_ref[c, leaf + b * N_LEAF] // N_FRONT * 2 + b - step * STEP_ROWS

            @pl.when((q >= 0) & (q < STEP_ROWS))
            def _():
                there = pl.ds(q * (8 * BLK) + s, BLK, stride=8)
                out_ref[there, :] = out_ref[there, :] + update_ref[c, b].astype(F32)

    @pl.when(front < KS)
    def _():
        column = pl.ds(pl.multiple_of(owner * BLK, BLK), BLK)
        for q, at in enumerate(order):
            out_ref[pl.ds(q * 8 * BLK, BLK, stride=8), :] = low_ref[at : at + BLK, column]

    @pl.when(step == 0)
    def _():
        out_ref[: 8 * BLK, :] = jnp.zeros((8 * BLK, BLK), F32)

        @pl.when(front < KS)
        def _():
            out_ref[pl.ds(0, BLK, stride=8), :] = l_ref[...]


def schur(child_map, low, given, upper, panels, m, cols, rows, front):
    steps = 16 // STEP_ROWS
    block = pl.BlockSpec((STEP_ROWS * BLK * 8, BLK), lambda i: (i, 0))
    return pl.pallas_call(
        schur_kernel,
        name="schur",
        grid=(steps,),
        out_shape=jax.ShapeDtypeStruct((16 * BLK * 8, BLK), F32),
        in_specs=[TABLE] + [WHOLE] * 4 + [pl.BlockSpec(memory_space=pltpu.HBM)] * 3 + [block],
        out_specs=block,
        scratch_shapes=[
            pltpu.VMEM((ORDER, ORDER), BF16),
            pltpu.VMEM((ORDER, ORDER), BF16),
            pltpu.VMEM((2, ORDER, ORDER), BF16),
            pltpu.VMEM((2, KS, 2 * BLK, BLK), BF16),
            pltpu.VMEM((ORDER, ORDER), BF16),
            pltpu.VMEM((STEP_ROWS * BLK, ORDER), F32),
            pltpu.VMEM((N_LEAF, 2, BLK, BLK), BF16),
            pltpu.SemaphoreType.DMA((5, KS)),
        ],
        compiler_params=pltpu.CompilerParams(vmem_limit_bytes=52 << 20),
    )(child_map, low, given, upper, panels, m, cols, rows, front)


def gather(x, axis, count):
    spread = jnp.broadcast_to(x[None], (count, *x.shape))
    return lax.all_to_all(spread, axis, 0, 0)


def exchange(flip):
    return [
        (a * N_FRONT + b * N_LEAF + c, c * N_FRONT + (b ^ flip) * N_LEAF + a)
        for a in range(N_LEAF)
        for b in range(2)
        for c in range(N_LEAF)
    ]


def front_pieces(first, leaf_id, front_id):
    z, x = front_id // 4, front_id % 4
    got = [
        lax.ppermute(first, "front", [(4 * i + j, (i + k) % 4 * 4 + j) for i in (0, 1) for j in range(4)])
        for k in (1, 2, 3)
    ]
    near = jnp.where(z == 0, first, jnp.where(z == 1, got[0], jnp.where(z == 2, got[1], got[2])))
    far = jnp.where(z == 0, got[2], jnp.where(z == 1, first, jnp.where(z == 2, got[0], got[1])))
    extra = jnp.where(leaf_id < 4, near[1], far[1])
    mine = jnp.stack([near[0], far[0], extra])
    every = [mine] + [
        lax.ppermute(mine, "front", [(4 * i + j, 4 * i + (j + k) % 4) for i in range(4) for j in range(4)])
        for k in (1, 2, 3)
    ]
    at = (x + 8 - leaf_id) % 4
    extra = every[0][2]
    for k in (1, 2, 3):
        extra = jnp.where(at == k, every[k][2], extra)
    return jnp.concatenate([one[:2] for one in every] + [extra[None]], axis=0)


def one_pass(front_entries, child_panels, child_blocks, child_map):
    front = front_entries.reshape(16 * BLK * 8, BLK)
    front_id = lax.axis_index("front")
    leaf_id = lax.axis_index("leaf")
    own = child_panels[0]
    halves_of = own.reshape(2, BLK // 2, own.shape[1])
    early = front_id < N_LEAF
    same = lax.ppermute(jnp.where(early, halves_of[0], halves_of[1]), MESH_AXES, exchange(0))
    other = lax.ppermute(jnp.where(early, halves_of[1], halves_of[0]), MESH_AXES, exchange(1))
    blocks = child_blocks[0].reshape(2, N_LEAF, BLK, BLK).transpose(1, 0, 2, 3)
    given = lax.all_to_all(blocks, "leaf", 0, 0)
    own, same, other, given = lax.optimization_barrier((own, same, other, given))
    panels = lax.all_gather(own, "leaf", axis=0)
    upper = gather(jnp.where(early, same, other), "front", N_FRONT)
    upper = upper.reshape(2, N_LEAF, BLK // 2, own.shape[1])
    lower = jnp.where(early, other, same).reshape(BLK // 2, 4, BLK).transpose(1, 0, 2)
    flat, turned, first = pivot_rows(child_map, front, given, upper, panels)
    cols = lax.all_gather(flat, "leaf", axis=0, tiled=True)
    turned = lax.ppermute(turned, MESH_AXES, exchange(0))
    whole = front_pieces(first, leaf_id, front_id)
    turned, whole = lax.optimization_barrier((turned, whole))
    separator = [whole] + [
        lax.ppermute(whole, "leaf", [(i, (i + k) % N_LEAF) for i in range(N_LEAF)])
        for k in range(1, N_LEAF)
    ]
    packed = jnp.concatenate([turned.reshape(ORDER, BLK), lower.reshape(2 * BLK, BLK)], axis=0)
    rows = lax.all_gather(packed, "front", axis=0)
    m, low = cholesky(separator)
    rows = rows.reshape(2, KS, ORDER + 2 * BLK, BLK)
    out = schur(child_map, low, given, upper, panels, m, cols, rows, front)
    return out.reshape(16, 1, BLK, 8, 1, BLK)


def solution(mesh):
    placed = (
        P(None, "leaf", None, None, "front", None),
        P("leaf", "front", None),
        P("leaf", None, "front"),
        P(),
    )
    return jax.shard_map(
        one_pass,
        mesh=mesh,
        in_specs=placed,
        out_specs=P(None, "leaf", None, None, "front", None),
        check_vma=False,
    )
```

```python
import jax
import jax.numpy as jnp
from jax import lax
from jax.experimental import pallas as pl
from jax.experimental.pallas import tpu as pltpu
from jax.sharding import PartitionSpec as P


F32 = jnp.float32
BF16 = jnp.bfloat16
KS = 8
BLK = 128
ORDER = KS * BLK
N_LEAF = 8
N_FRONT = 16
STEP_ROWS = 4
MESH_AXES = ("leaf", "front")
CORES = [(i, i ^ 1) for i in range(N_LEAF)]
WHOLE = pl.BlockSpec(memory_space=pltpu.VMEM)
TABLE = pl.BlockSpec(memory_space=pltpu.SMEM)


def dot(a, b, ca, cb, precision=None):
    return lax.dot_general(
        a, b, (((ca,), (cb,)), ((), ())), precision=precision, preferred_element_type=F32
    )


def place():
    return lax.axis_index("leaf"), lax.axis_index("front")


def rows_of(rows_ref, c):
    return jnp.concatenate([rows_ref[0, c], rows_ref[1, c]], axis=0)


def update_of(given, left, right):
    return (given.astype(F32) - dot(left, right, 1, 1)).astype(BF16)


def pivot_kernel(
    map_ref, front_ref, given_ref, rows_ref, cols_ref, flat_ref, turned_ref, first_ref, sum_ref
):
    leaf, front = place()
    for s in range(8):
        sum_ref[:, s * BLK : (s + 1) * BLK] = front_ref[pl.ds(s, BLK, stride=8), :]
    for c in range(N_LEAF):
        cycle = map_ref[c, front] // N_FRONT

        @pl.when(map_ref[c, leaf] // N_FRONT == 0)
        def _():
            cols = pl.ds(pl.multiple_of(cycle * BLK, BLK), BLK)
            update = update_of(given_ref[c, 0], rows_of(rows_ref, c), cols_ref[c])
            sum_ref[:, cols] += update.astype(F32)

    flat_ref[...] = sum_ref[...].astype(BF16)
    for s in range(8):
        turned_ref[s] = jnp.transpose(sum_ref[:, s * BLK : (s + 1) * BLK]).astype(BF16)
    half = BLK // 2
    bottom = sum_ref[half:, :BLK]
    top = jnp.where(leaf > front, jnp.transpose(sum_ref[:, :BLK])[:half], sum_ref[:half, :BLK])
    first_ref[0] = jnp.where(leaf < front, bottom, top).astype(BF16)
    first_ref[1] = bottom.astype(BF16)


def pivot_rows(child_map, front, given, rows, cols):
    return pl.pallas_call(
        pivot_kernel,
        name="pivot_rows",
        grid=(1,),
        out_shape=(
            jax.ShapeDtypeStruct((BLK, 8 * BLK), BF16),
            jax.ShapeDtypeStruct((8, BLK, BLK), BF16),
            jax.ShapeDtypeStruct((2, BLK // 2, BLK), BF16),
        ),
        in_specs=[
            TABLE,
            pl.BlockSpec((8 * BLK, BLK), lambda i: (0, 0)),
            pl.BlockSpec((N_LEAF, 1, BLK, BLK), lambda i: (0, 0, 0, 0)),
            pl.BlockSpec(rows.shape, lambda i: (0, 0, 0, 0)),
            pl.BlockSpec(cols.shape, lambda i: (0, 0, 0)),
        ],
        out_specs=(
            pl.BlockSpec((BLK, 8 * BLK), lambda i: (0, 0)),
            pl.BlockSpec((8, BLK, BLK), lambda i: (0, 0, 0)),
            pl.BlockSpec((2, BLK // 2, BLK), lambda i: (0, 0, 0)),
        ),
        scratch_shapes=[pltpu.VMEM((BLK, 8 * BLK), F32)],
    )(child_map, front, given, rows, cols)


def lanes(x, j):
    return jnp.broadcast_to(x[:, j : j + 1], (8, BLK))


def spread(ref, i):
    return ref[pl.ds(i, 8, stride=0), :]


def sum_products(v, r):
    t = [v[i] * r[i] for i in range(8)]
    while len(t) > 1:
        t = [t[i] + t[i + 1] for i in range(0, len(t), 2)]
    return t[0]


def high_part(x):
    return x.astype(BF16).astype(F32)


def factor(g_ref, e_ref, c_ref):
    for p in range(16):
        rows = pl.ds(8 * p, 8)
        below = pl.ds(8 * p + 8, 8)
        top = g_ref[rows, :]
        slot = p % 2 * 64
        for j in range(8):
            c_ref[slot + 8 * j : slot + 8 * j + 8, :] = lanes(top, 8 * p + j)
        a = [
            [spread(c_ref, slot + 8 * j + i) if j <= i else None for j in range(8)]
            for i in range(8)
        ]
        r = [spread(g_ref, 8 * p + i) for i in range(8)]
        e = [spread(e_ref, 8 * p + i) for i in range(8)]
        more = p < 15
        if more:
            after = g_ref[below, :]
            v = [lanes(after, 8 * p + j) for j in range(8)]
        for j in range(8):
            if j % 2 == 0:
                corner = a[j + 1][j + 1] * a[j][j] - a[j + 1][j] * a[j + 1][j]
                inv = lax.rsqrt(a[j][j])
                second = lax.rsqrt(corner) * (a[j][j] * inv)
            else:
                inv = second
            r[j] = r[j] * inv
            e[j] = e[j] * inv
            if more:
                v[j] = v[j] * inv
            col = [None] * 8
            for i in range(j + 1, 8):
                col[i] = a[i][j] * inv
            for i in range(j + 1, 8):
                for k in range(j + 1, i + 1):
                    if j % 2 or i > j + 1:
                        a[i][k] = a[i][k] - col[i] * col[k]
            for i in range(j + 1, 8):
                r[i] = r[i] - col[i] * r[j]
                e[i] = e[i] - col[i] * e[j]
                if more:
                    v[i] = v[i] - col[i] * v[j]
        if more:
            g_ref[below, :] = after - sum_products(v, r)
            e_ref[below, :] = e_ref[below, :] - sum_products(v, e)
        sub = lax.broadcasted_iota(jnp.int32, (8, BLK), 0)
        u, w = r[0], e[0]
        for i in range(1, 8):
            u = jnp.where(sub == i, r[i], u)
            w = jnp.where(sub == i, e[i], w)
        g_ref[rows, :] = u
        e_ref[rows, :] = w
        if p < 14:
            turned = jnp.transpose(u)[8 * p + 16 : 8 * p + 24, :]
            vg = [lanes(turned, i) for i in range(8)]
            there = pl.ds(8 * p + 16, 8)
            g_ref[there, :] = g_ref[there, :] - sum_products(vg, r)
            e_ref[there, :] = e_ref[there, :] - sum_products(vg, e)
        if p < 13:
            uh, wh = high_part(u), high_part(w)
            ul, wl = u - uh, w - wh
            left = jnp.concatenate([uh, uh, ul, ul], axis=0).astype(BF16)
            top = jnp.concatenate([uh, wh], axis=1)
            low = jnp.concatenate([ul, wl], axis=1)
            right = jnp.concatenate([top, low, top, low], axis=0).astype(BF16)
            both = dot(left, right, 0, 0)
            there = slice(8 * p + 24, BLK)
            g_ref[there, :] = g_ref[there, :] - both[there, :BLK]
            e_ref[there, :] = e_ref[there, :] - both[there, BLK:]


def halves(x):
    high = x.astype(BF16)
    return high, (x - high.astype(F32)).astype(BF16)


def cholesky_kernel(
    *refs
):
    piece_refs, refs = refs[:N_LEAF], refs[N_LEAF:]
    (m_hbm, l_ref, s_ref, d_ref, g_ref, e_ref, nl_ref, nr_ref, m_ref, c_ref, sem) = refs
    leaf, front = place()
    half = BLK // 2
    for k in range(N_LEAF):
        near = leaf if k < 4 else leaf + 1 - 2 * (leaf % 2)
        giver = (near + N_LEAF - 2 * (k % 4)) % N_LEAF * BLK
        for n in range(KS + 1):
            at = (n % 2 * 4 + (front + 4 - n // 2) % 4) * BLK
            top = at <= giver
            row = jnp.where(top, at, giver + half) if n < KS else giver + half
            col = jnp.where(top, giver, at) if n < KS else giver
            rows = pl.ds(pl.multiple_of(row, half), half)
            s_ref[rows, pl.ds(pl.multiple_of(col, BLK), BLK)] = piece_refs[k][n].astype(F32)
    row_id = lax.broadcasted_iota(jnp.int32, (BLK, BLK), 0)
    col_id = lax.broadcasted_iota(jnp.int32, (BLK, BLK), 1)
    ident = (row_id == col_id).astype(F32)

    @pl.loop(0, KS)
    def _(k):
        here = pl.ds(pl.multiple_of(k * BLK, BLK), BLK)
        g_ref[...] = s_ref[here, here]
        e_ref[...] = ident
        factor(g_ref, e_ref, c_ref)
        d_ref[here, :] = g_ref[...]
        s_ref[here, here] = ident
        eh, el = halves(e_ref[...])
        sh, sl = halves(s_ref[here, :])
        left = jnp.concatenate([eh, el, eh], axis=1)
        row = dot(left, jnp.concatenate([sh, sh, sl], axis=0), 1, 0)
        s_ref[here, :] = row
        high, low = halves(row)
        for n in range(3):
            part = slice(n * BLK, (n + 1) * BLK)
            nl_ref[part, :] = low if n == 1 else high
            nr_ref[part, :] = low if n == 2 else high
        keep = lax.broadcasted_iota(jnp.int32, (BLK, ORDER), 1) < (k + 1) * BLK
        m_ref[here, :] = jnp.where(keep, row, 0.0).astype(BF16)

        @pl.loop(k + 1, KS)
        def _(i):
            there = pl.ds(pl.multiple_of(i * BLK, BLK), BLK)
            s_ref[there, here] = jnp.zeros((BLK, BLK), F32)
            s_ref[there, :] = s_ref[there, :] - dot(nl_ref[:, there], nr_ref[...], 0, 0)

    out = pltpu.make_async_copy(m_ref, m_hbm, sem)
    out.start()
    front = jnp.minimum(front, KS - 1)
    mine = pl.ds(pl.multiple_of(leaf * BLK, BLK), BLK)
    other = pl.ds(pl.multiple_of(front * BLK, BLK), BLK)
    upper = jnp.where(row_id <= col_id, d_ref[mine, :], 0.0)
    beyond = jnp.where(front < leaf, s_ref[other, mine], 0.0)
    l_ref[...] = jnp.transpose(jnp.where(front == leaf, upper, beyond))
    out.wait()


def cholesky(pieces):
    return pl.pallas_call(
        cholesky_kernel,
        name="cholesky",
        out_shape=(
            jax.ShapeDtypeStruct((ORDER, ORDER), BF16),
            jax.ShapeDtypeStruct((BLK, BLK), F32),
        ),
        in_specs=[WHOLE] * N_LEAF,
        out_specs=(pl.BlockSpec(memory_space=pltpu.HBM), WHOLE),
        scratch_shapes=[
            pltpu.VMEM((ORDER, ORDER), F32),
            pltpu.VMEM((ORDER, BLK), F32),
            pltpu.VMEM((BLK, BLK), F32),
            pltpu.VMEM((BLK, BLK), F32),
            pltpu.VMEM((3 * BLK, ORDER), BF16),
            pltpu.VMEM((3 * BLK, ORDER), BF16),
            pltpu.VMEM((ORDER, ORDER), BF16),
            pltpu.VMEM((BLK, BLK), F32),
            pltpu.SemaphoreType.DMA,
        ],
        compiler_params=pltpu.CompilerParams(vmem_limit_bytes=52 << 20),
        cost_estimate=pl.CostEstimate(
            flops=60_000_000_000, bytes_accessed=6 << 20, transcendentals=1024
        ),
    )(*pieces)


def columns_kernel(m_ref, cols_ref, given_ref, upper_ref, panel_ref, w_ref, early_ref):
    for n in range(4):
        take = slice(n * 256, (n + 1) * 256)
        upto = slice(0, (n + 1) * 256)
        w_ref[take, :] = dot(m_ref[take, upto], cols_ref[upto, :], 1, 0).astype(BF16)
    for c in range(N_LEAF):
        early_ref[c] = update_of(given_ref[c, 0], rows_of(upper_ref, c), panel_ref[c])


def columns(m, cols, given, upper, panels):
    return pl.pallas_call(
        columns_kernel,
        name="columns",
        grid=(1,),
        out_shape=(
            jax.ShapeDtypeStruct((ORDER, ORDER), BF16),
            jax.ShapeDtypeStruct((N_LEAF, BLK, BLK), BF16),
        ),
        in_specs=[
            WHOLE,
            WHOLE,
            pl.BlockSpec((N_LEAF, 1, BLK, BLK), lambda i: (0, 0, 0, 0)),
            WHOLE,
            WHOLE,
        ],
        out_specs=(WHOLE, WHOLE),
        compiler_params=pltpu.CompilerParams(vmem_limit_bytes=52 << 20),
        cost_estimate=pl.CostEstimate(
            flops=4_000_000_000, bytes_accessed=8 << 20, transcendentals=0
        ),
    )(m, cols, given, upper, panels)


def schur_kernel(
    map_ref, l_ref, given_ref, early_ref, panel_ref, w_ref, m_hbm, rows_hbm, front_ref,
    out_ref, m_ref, rows_ref, lower_ref, low_ref, late_ref, sem
):
    step = pl.program_id(0)
    leaf, front = place()
    owner = jnp.minimum(front, KS - 1)

    def copies():
        yield pltpu.make_async_copy(m_hbm, m_ref, sem.at[2, 0])
        for b in range(2):
            for a in range(KS):
                columns = pl.ds(a * BLK, BLK)
                source = rows_hbm.at[b, a]
                yield pltpu.make_async_copy(
                    source.at[pl.ds(0, ORDER)], rows_ref.at[b, :, columns], sem.at[b, a]
                )
                yield pltpu.make_async_copy(
                    source.at[pl.ds(ORDER, 2 * BLK)], lower_ref.at[b, a], sem.at[3 + b, a]
                )

    @pl.when(step == 0)
    def _():
        for copy in copies():
            copy.start()
        for copy in copies():
            copy.wait()
        for c in range(N_LEAF):
            product = jnp.zeros((BLK, BLK), F32)
            for n in range(4):
                part = slice(n * BLK // 2, (n + 1) * BLK // 2)
                rows = jnp.concatenate([lower_ref[0, c, part], lower_ref[1, c, part]], axis=0)
                product += dot(rows, panel_ref[c, :, n * BLK : (n + 1) * BLK], 1, 1)
            late_ref[c] = (given_ref[c, 0].astype(F32) - product).astype(BF16)

    pair = STEP_ROWS // 2 * BLK
    source = pl.ds(pl.multiple_of(step * pair, pair), pair)
    for n in range(4):
        take = slice(n * 256, (n + 1) * 256)
        upto = slice(0, (n + 1) * 256)
        both = jnp.concatenate([rows_ref[0, source, upto], rows_ref[1, source, upto]], axis=0)
        low_ref[:, take] = dot(both, m_ref[take, upto], 1, 1)
    low = low_ref[...].astype(BF16)
    order = [q % 2 * pair + q // 2 * BLK for q in range(STEP_ROWS)]
    for n in range(4):
        part = dot(low, w_ref[:, n * 256 : (n + 1) * 256], 1, 0)
        for s in range(2):
            for q, at in enumerate(order):
                there = pl.ds(q * 8 * BLK + 2 * n + s, BLK, stride=8)
                product = part[at : at + BLK, s * BLK : (s + 1) * BLK]
                out_ref[there, :] = front_ref[there, :] - product
    for c in range(N_LEAF):
        s = map_ref[c, front] // N_FRONT
        for b in range(2):
            q = map_ref[c, leaf + b * N_LEAF] // N_FRONT * 2 + b - step * STEP_ROWS

            @pl.when((q >= 0) & (q < STEP_ROWS))
            def _():
                there = pl.ds(q * (8 * BLK) + s, BLK, stride=8)
                added = (late_ref if b else early_ref)[c].astype(F32)
                out_ref[there, :] = out_ref[there, :] + added

    @pl.when(front < KS)
    def _():
        column = pl.ds(pl.multiple_of(owner * BLK, BLK), BLK)
        for q, at in enumerate(order):
            out_ref[pl.ds(q * 8 * BLK, BLK, stride=8), :] = low_ref[at : at + BLK, column]

    @pl.when(step == 0)
    def _():
        out_ref[: 8 * BLK, :] = jnp.zeros((8 * BLK, BLK), F32)

        @pl.when(front < KS)
        def _():
            out_ref[pl.ds(0, BLK, stride=8), :] = l_ref[...]


def schur(child_map, low, given, early, panels, w, m, rows, front):
    steps = 16 // STEP_ROWS
    block = pl.BlockSpec((STEP_ROWS * BLK * 8, BLK), lambda i: (i, 0))
    return pl.pallas_call(
        schur_kernel,
        name="schur",
        grid=(steps,),
        out_shape=jax.ShapeDtypeStruct((16 * BLK * 8, BLK), F32),
        in_specs=[
            TABLE,
            WHOLE,
            pl.BlockSpec((N_LEAF, 1, BLK, BLK), lambda i: (0, 1, 0, 0)),
            WHOLE,
            WHOLE,
            WHOLE,
            pl.BlockSpec(memory_space=pltpu.HBM),
            pl.BlockSpec(memory_space=pltpu.HBM),
            block,
        ],
        out_specs=block,
        scratch_shapes=[
            pltpu.VMEM((ORDER, ORDER), BF16),
            pltpu.VMEM((2, ORDER, ORDER), BF16),
            pltpu.VMEM((2, KS, 2 * BLK, BLK), BF16),
            pltpu.VMEM((STEP_ROWS * BLK, ORDER), F32),
            pltpu.VMEM((N_LEAF, BLK, BLK), BF16),
            pltpu.SemaphoreType.DMA((5, KS)),
        ],
        compiler_params=pltpu.CompilerParams(vmem_limit_bytes=52 << 20),
    )(child_map, low, given, early, panels, w, m, rows, front)


def gather(x, axis, count):
    spread = jnp.broadcast_to(x[None], (count, *x.shape))
    return lax.all_to_all(spread, axis, 0, 0)


def exchange(flip):
    return [
        (a * N_FRONT + b * N_LEAF + c, c * N_FRONT + (b ^ flip) * N_LEAF + a)
        for a in range(N_LEAF)
        for b in range(2)
        for c in range(N_LEAF)
    ]


def front_pieces(first, leaf_id, front_id):
    z, x = front_id // 4, front_id % 4
    got = [
        lax.ppermute(first, "front", [(4 * i + j, (i + k) % 4 * 4 + j) for i in (0, 1) for j in range(4)])
        for k in (1, 2, 3)
    ]
    near = jnp.where(z == 0, first, jnp.where(z == 1, got[0], jnp.where(z == 2, got[1], got[2])))
    far = jnp.where(z == 0, got[2], jnp.where(z == 1, first, jnp.where(z == 2, got[0], got[1])))
    extra = jnp.where(leaf_id < 4, near[1], far[1])
    mine = jnp.stack([near[0], far[0], extra])
    every = [mine] + [
        lax.ppermute(mine, "front", [(4 * i + j, 4 * i + (j + k) % 4) for i in range(4) for j in range(4)])
        for k in (1, 2, 3)
    ]
    at = (x + 8 - leaf_id) % 4
    extra = every[0][2]
    for k in (1, 2, 3):
        extra = jnp.where(at == k, every[k][2], extra)
    return jnp.concatenate([one[:2] for one in every] + [extra[None]], axis=0)


def one_pass(front_entries, child_panels, child_blocks, child_map):
    front = front_entries.reshape(16 * BLK * 8, BLK)
    front_id = lax.axis_index("front")
    leaf_id = lax.axis_index("leaf")
    own = child_panels[0]
    halves_of = own.reshape(2, BLK // 2, own.shape[1])
    early = front_id < N_LEAF
    same = lax.ppermute(jnp.where(early, halves_of[0], halves_of[1]), MESH_AXES, exchange(0))
    other = lax.ppermute(jnp.where(early, halves_of[1], halves_of[0]), MESH_AXES, exchange(1))
    blocks = child_blocks[0].reshape(2, N_LEAF, BLK, BLK).transpose(1, 0, 2, 3)
    given = lax.all_to_all(blocks, "leaf", 0, 0)
    own, same, other, given = lax.optimization_barrier((own, same, other, given))
    panels = lax.all_gather(own, "leaf", axis=0)
    upper = gather(jnp.where(early, same, other), "front", N_FRONT)
    upper = upper.reshape(2, N_LEAF, BLK // 2, own.shape[1])
    lower = jnp.where(early, other, same).reshape(BLK // 2, 4, BLK).transpose(1, 0, 2)
    flat, turned, first = pivot_rows(child_map, front, given, upper, panels)
    cols = lax.all_gather(flat, "leaf", axis=0, tiled=True)
    turned = lax.ppermute(turned, MESH_AXES, exchange(0))
    whole = front_pieces(first, leaf_id, front_id)
    turned, whole = lax.optimization_barrier((turned, whole))
    across = [lax.ppermute(whole, "leaf", CORES)]
    along = [whole] + [
        lax.ppermute(whole, "leaf", [(i, (i + 2 * k) % N_LEAF) for i in range(N_LEAF)])
        for k in (1, 2, 3)
    ]
    across += [lax.ppermute(one, "leaf", CORES) for one in along[1:]]
    separator = along + across
    packed = jnp.concatenate([turned.reshape(ORDER, BLK), lower.reshape(2 * BLK, BLK)], axis=0)
    rows = lax.all_gather(packed, "front", axis=0)
    m, low = cholesky(separator)
    rows = rows.reshape(2, KS, ORDER + 2 * BLK, BLK)
    w, early_updates = columns(m, cols, given, upper, panels)
    out = schur(child_map, low, given, early_updates, panels, w, m, rows, front)
    return out.reshape(16, 1, BLK, 8, 1, BLK)


def solution(mesh):
    placed = (
        P(None, "leaf", None, None, "front", None),
        P("leaf", "front", None),
        P("leaf", None, "front"),
        P(),
    )
    return jax.shard_map(
        one_pass,
        mesh=mesh,
        in_specs=placed,
        out_specs=P(None, "leaf", None, None, "front", None),
        check_vma=False,
    )
```

```python
import jax
import jax.numpy as jnp
from jax import lax
from jax.experimental import pallas as pl
from jax.experimental.pallas import tpu as pltpu
from jax.sharding import PartitionSpec as P


F32 = jnp.float32
BF16 = jnp.bfloat16
KS = 8
BLK = 128
ORDER = KS * BLK
N_LEAF = 8
N_FRONT = 16
STEP_ROWS = 4
MESH_AXES = ("leaf", "front")
CORES = [(i, i ^ 1) for i in range(N_LEAF)]
WHOLE = pl.BlockSpec(memory_space=pltpu.VMEM)
TABLE = pl.BlockSpec(memory_space=pltpu.SMEM)


def dot(a, b, ca, cb, precision=None):
    return lax.dot_general(
        a, b, (((ca,), (cb,)), ((), ())), precision=precision, preferred_element_type=F32
    )


def place():
    return lax.axis_index("leaf"), lax.axis_index("front")


def rows_of(rows_ref, c):
    return jnp.concatenate([rows_ref[0, c], rows_ref[1, c]], axis=0)


def update_of(given, left, right):
    return (given.astype(F32) - dot(left, right, 1, 1)).astype(BF16)


def pivot_kernel(
    map_ref, front_ref, given_ref, rows_ref, cols_ref, flat_ref, turned_ref, first_ref, sum_ref
):
    leaf, front = place()
    for s in range(8):
        sum_ref[:, s * BLK : (s + 1) * BLK] = front_ref[pl.ds(s, BLK, stride=8), :]
    for c in range(N_LEAF):
        cycle = map_ref[c, front] // N_FRONT

        @pl.when(map_ref[c, leaf] // N_FRONT == 0)
        def _():
            cols = pl.ds(pl.multiple_of(cycle * BLK, BLK), BLK)
            update = update_of(given_ref[c, 0], rows_of(rows_ref, c), cols_ref[c])
            sum_ref[:, cols] += update.astype(F32)

    flat_ref[...] = sum_ref[...].astype(BF16)
    for s in range(8):
        turned_ref[s] = jnp.transpose(sum_ref[:, s * BLK : (s + 1) * BLK]).astype(BF16)
    half = BLK // 2
    bottom = sum_ref[half:, :BLK]
    top = jnp.where(leaf > front, jnp.transpose(sum_ref[:, :BLK])[:half], sum_ref[:half, :BLK])
    first_ref[0] = jnp.where(leaf < front, bottom, top).astype(BF16)
    first_ref[1] = bottom.astype(BF16)


def pivot_rows(child_map, front, given, rows, cols):
    return pl.pallas_call(
        pivot_kernel,
        name="pivot_rows",
        grid=(1,),
        out_shape=(
            jax.ShapeDtypeStruct((BLK, 8 * BLK), BF16),
            jax.ShapeDtypeStruct((8, BLK, BLK), BF16),
            jax.ShapeDtypeStruct((2, BLK // 2, BLK), BF16),
        ),
        in_specs=[
            TABLE,
            pl.BlockSpec((8 * BLK, BLK), lambda i: (0, 0)),
            pl.BlockSpec((N_LEAF, 1, BLK, BLK), lambda i: (0, 0, 0, 0)),
            pl.BlockSpec(rows.shape, lambda i: (0, 0, 0, 0)),
            pl.BlockSpec(cols.shape, lambda i: (0, 0, 0)),
        ],
        out_specs=(
            pl.BlockSpec((BLK, 8 * BLK), lambda i: (0, 0)),
            pl.BlockSpec((8, BLK, BLK), lambda i: (0, 0, 0)),
            pl.BlockSpec((2, BLK // 2, BLK), lambda i: (0, 0, 0)),
        ),
        scratch_shapes=[pltpu.VMEM((BLK, 8 * BLK), F32)],
    )(child_map, front, given, rows, cols)


def lanes(x, j):
    return jnp.broadcast_to(x[:, j : j + 1], (8, BLK))


def spread(ref, i):
    return ref[pl.ds(i, 8, stride=0), :]


def sum_products(v, r):
    t = [v[i] * r[i] for i in range(8)]
    while len(t) > 1:
        t = [t[i] + t[i + 1] for i in range(0, len(t), 2)]
    return t[0]


def high_part(x):
    return x.astype(BF16).astype(F32)


def factor(g_ref, e_ref, c_ref):
    for p in range(16):
        rows = pl.ds(8 * p, 8)
        below = pl.ds(8 * p + 8, 8)
        top = g_ref[rows, :]
        slot = p % 2 * 64
        for j in range(8):
            c_ref[slot + 8 * j : slot + 8 * j + 8, :] = lanes(top, 8 * p + j)
        a = [
            [spread(c_ref, slot + 8 * j + i) if j <= i else None for j in range(8)]
            for i in range(8)
        ]
        r = [spread(g_ref, 8 * p + i) for i in range(8)]
        e = [spread(e_ref, 8 * p + i) for i in range(8)]
        more = p < 15
        if more:
            after = g_ref[below, :]
            v = [lanes(after, 8 * p + j) for j in range(8)]
        for j in range(8):
            if j % 2 == 0:
                corner = a[j + 1][j + 1] * a[j][j] - a[j + 1][j] * a[j + 1][j]
                inv = lax.rsqrt(a[j][j])
                second = lax.rsqrt(corner) * (a[j][j] * inv)
            else:
                inv = second
            r[j] = r[j] * inv
            e[j] = e[j] * inv
            if more:
                v[j] = v[j] * inv
            col = [None] * 8
            for i in range(j + 1, 8):
                col[i] = a[i][j] * inv
            for i in range(j + 1, 8):
                for k in range(j + 1, i + 1):
                    if j % 2 or i > j + 1:
                        a[i][k] = a[i][k] - col[i] * col[k]
            for i in range(j + 1, 8):
                r[i] = r[i] - col[i] * r[j]
                e[i] = e[i] - col[i] * e[j]
                if more:
                    v[i] = v[i] - col[i] * v[j]
        if more:
            g_ref[below, :] = after - sum_products(v, r)
            e_ref[below, :] = e_ref[below, :] - sum_products(v, e)
        sub = lax.broadcasted_iota(jnp.int32, (8, BLK), 0)
        u, w = r[0], e[0]
        for i in range(1, 8):
            u = jnp.where(sub == i, r[i], u)
            w = jnp.where(sub == i, e[i], w)
        g_ref[rows, :] = u
        e_ref[rows, :] = w
        if p < 14:
            turned = jnp.transpose(u)[8 * p + 16 : 8 * p + 24, :]
            vg = [lanes(turned, i) for i in range(8)]
            there = pl.ds(8 * p + 16, 8)
            g_ref[there, :] = g_ref[there, :] - sum_products(vg, r)
            e_ref[there, :] = e_ref[there, :] - sum_products(vg, e)
        if p < 13:
            uh, wh = high_part(u), high_part(w)
            ul, wl = u - uh, w - wh
            left = jnp.concatenate([uh, uh, ul, ul], axis=0).astype(BF16)
            top = jnp.concatenate([uh, wh], axis=1)
            low = jnp.concatenate([ul, wl], axis=1)
            right = jnp.concatenate([top, low, top, low], axis=0).astype(BF16)
            both = dot(left, right, 0, 0)
            there = slice(8 * p + 24, BLK)
            g_ref[there, :] = g_ref[there, :] - both[there, :BLK]
            e_ref[there, :] = e_ref[there, :] - both[there, BLK:]


def halves(x):
    high = x.astype(BF16)
    return high, (x - high.astype(F32)).astype(BF16)


def cholesky_kernel(
    *refs
):
    piece_refs, refs = refs[:N_LEAF], refs[N_LEAF:]
    (m_hbm, l_ref, s_ref, d_ref, g_ref, e_ref, nl_ref, nr_ref, m_ref, c_ref, sem) = refs
    leaf, front = place()
    half = BLK // 2
    for k in range(N_LEAF):
        near = leaf if k < 4 else leaf + 1 - 2 * (leaf % 2)
        giver = (near + N_LEAF - 2 * (k % 4)) % N_LEAF * BLK
        for n in range(KS + 1):
            at = (n % 2 * 4 + (front + 4 - n // 2) % 4) * BLK
            top = at <= giver
            row = jnp.where(top, at, giver + half) if n < KS else giver + half
            col = jnp.where(top, giver, at) if n < KS else giver
            rows = pl.ds(pl.multiple_of(row, half), half)
            s_ref[rows, pl.ds(pl.multiple_of(col, BLK), BLK)] = piece_refs[k][n].astype(F32)
    row_id = lax.broadcasted_iota(jnp.int32, (BLK, BLK), 0)
    col_id = lax.broadcasted_iota(jnp.int32, (BLK, BLK), 1)
    ident = (row_id == col_id).astype(F32)

    @pl.loop(0, KS)
    def _(k):
        here = pl.ds(pl.multiple_of(k * BLK, BLK), BLK)
        g_ref[...] = s_ref[here, here]
        e_ref[...] = ident
        factor(g_ref, e_ref, c_ref)
        d_ref[here, :] = g_ref[...]
        s_ref[here, here] = ident
        eh, el = halves(e_ref[...])
        sh, sl = halves(s_ref[here, :])
        left = jnp.concatenate([eh, el, eh], axis=1)
        row = dot(left, jnp.concatenate([sh, sh, sl], axis=0), 1, 0)
        s_ref[here, :] = row
        high, low = halves(row)
        for n in range(3):
            part = slice(n * BLK, (n + 1) * BLK)
            nl_ref[part, :] = low if n == 1 else high
            nr_ref[part, :] = low if n == 2 else high
        keep = lax.broadcasted_iota(jnp.int32, (BLK, ORDER), 1) < (k + 1) * BLK
        m_ref[here, :] = jnp.where(keep, row, 0.0).astype(BF16)

        @pl.loop(k + 1, KS)
        def _(i):
            there = pl.ds(pl.multiple_of(i * BLK, BLK), BLK)
            s_ref[there, here] = jnp.zeros((BLK, BLK), F32)
            s_ref[there, :] = s_ref[there, :] - dot(nl_ref[:, there], nr_ref[...], 0, 0)

    out = pltpu.make_async_copy(m_ref, m_hbm, sem)
    out.start()
    front = jnp.minimum(front, KS - 1)
    mine = pl.ds(pl.multiple_of(leaf * BLK, BLK), BLK)
    other = pl.ds(pl.multiple_of(front * BLK, BLK), BLK)
    upper = jnp.where(row_id <= col_id, d_ref[mine, :], 0.0)
    beyond = jnp.where(front < leaf, s_ref[other, mine], 0.0)
    l_ref[...] = jnp.transpose(jnp.where(front == leaf, upper, beyond))
    out.wait()


def cholesky(pieces):
    return pl.pallas_call(
        cholesky_kernel,
        name="cholesky",
        out_shape=(
            jax.ShapeDtypeStruct((ORDER, ORDER), BF16),
            jax.ShapeDtypeStruct((BLK, BLK), F32),
        ),
        in_specs=[WHOLE] * N_LEAF,
        out_specs=(pl.BlockSpec(memory_space=pltpu.HBM), WHOLE),
        scratch_shapes=[
            pltpu.VMEM((ORDER, ORDER), F32),
            pltpu.VMEM((ORDER, BLK), F32),
            pltpu.VMEM((BLK, BLK), F32),
            pltpu.VMEM((BLK, BLK), F32),
            pltpu.VMEM((3 * BLK, ORDER), BF16),
            pltpu.VMEM((3 * BLK, ORDER), BF16),
            pltpu.VMEM((ORDER, ORDER), BF16),
            pltpu.VMEM((BLK, BLK), F32),
            pltpu.SemaphoreType.DMA,
        ],
        compiler_params=pltpu.CompilerParams(vmem_limit_bytes=52 << 20),
        cost_estimate=pl.CostEstimate(
            flops=60_000_000_000, bytes_accessed=6 << 20, transcendentals=1024
        ),
    )(*pieces)


def columns_kernel(m_ref, cols_ref, given_ref, upper_ref, panel_ref, w_ref, early_ref):
    for n in range(4):
        take = slice(n * 256, (n + 1) * 256)
        upto = slice(0, (n + 1) * 256)
        w_ref[take, :] = dot(m_ref[take, upto], cols_ref[upto, :], 1, 0).astype(BF16)
    for c in range(N_LEAF):
        early_ref[c] = update_of(given_ref[c, 0], rows_of(upper_ref, c), panel_ref[c])


def columns(m, cols, given, upper, panels):
    return pl.pallas_call(
        columns_kernel,
        name="columns",
        grid=(1,),
        out_shape=(
            jax.ShapeDtypeStruct((ORDER, ORDER), BF16),
            jax.ShapeDtypeStruct((N_LEAF, BLK, BLK), BF16),
        ),
        in_specs=[
            WHOLE,
            WHOLE,
            pl.BlockSpec((N_LEAF, 1, BLK, BLK), lambda i: (0, 0, 0, 0)),
            WHOLE,
            WHOLE,
        ],
        out_specs=(WHOLE, WHOLE),
        compiler_params=pltpu.CompilerParams(vmem_limit_bytes=52 << 20),
        cost_estimate=pl.CostEstimate(
            flops=4_000_000_000, bytes_accessed=8 << 20, transcendentals=0
        ),
    )(m, cols, given, upper, panels)


def schur_kernel(
    map_ref, l_ref, given_ref, early_ref, panel_ref, w_ref, m_hbm, rows_hbm, front_ref,
    out_ref, m_ref, rows_ref, lower_ref, low_ref, late_ref, sem, late_sem, m_sem
):
    step = pl.program_id(0)
    leaf, front = place()
    owner = jnp.minimum(front, KS - 1)

    pair = STEP_ROWS // 2 * BLK

    def row_copies(turn):
        for b in range(2):
            for a in range(KS):
                here = pl.ds(pl.multiple_of(turn * pair, pair), pair)
                yield pltpu.make_async_copy(
                    rows_hbm.at[b, a, here],
                    rows_ref.at[b, here, pl.ds(a * BLK, BLK)],
                    sem.at[turn, b * KS + a],
                )

    def late_copies():
        for b in range(2):
            for a in range(KS):
                yield pltpu.make_async_copy(
                    rows_hbm.at[b, a, pl.ds(ORDER, 2 * BLK)], lower_ref.at[b, a], late_sem.at[b, a]
                )

    inverse = pltpu.make_async_copy(m_hbm, m_ref, m_sem)

    @pl.when(step == 0)
    def _():
        for copy in [inverse, *row_copies(0), *late_copies()]:
            copy.start()
        for turn in range(1, 16 // STEP_ROWS):
            for copy in row_copies(turn):
                copy.start()
        inverse.wait()

    for copy in row_copies(step):
        copy.wait()

    @pl.when(step == 0)
    def _():
        for copy in late_copies():
            copy.wait()
        for c in range(N_LEAF):
            product = jnp.zeros((BLK, BLK), F32)
            for n in range(4):
                part = slice(n * BLK // 2, (n + 1) * BLK // 2)
                rows = jnp.concatenate([lower_ref[0, c, part], lower_ref[1, c, part]], axis=0)
                product += dot(rows, panel_ref[c, :, n * BLK : (n + 1) * BLK], 1, 1)
            late_ref[c] = (given_ref[c, 0].astype(F32) - product).astype(BF16)

    source = pl.ds(pl.multiple_of(step * pair, pair), pair)
    for n in range(4):
        take = slice(n * 256, (n + 1) * 256)
        upto = slice(0, (n + 1) * 256)
        both = jnp.concatenate([rows_ref[0, source, upto], rows_ref[1, source, upto]], axis=0)
        low_ref[:, take] = dot(both, m_ref[take, upto], 1, 1)
    low = low_ref[...].astype(BF16)
    order = [q % 2 * pair + q // 2 * BLK for q in range(STEP_ROWS)]
    for n in range(4):
        part = dot(low, w_ref[:, n * 256 : (n + 1) * 256], 1, 0)
        for s in range(2):
            for q, at in enumerate(order):
                there = pl.ds(q * 8 * BLK + 2 * n + s, BLK, stride=8)
                product = part[at : at + BLK, s * BLK : (s + 1) * BLK]
                out_ref[there, :] = front_ref[there, :] - product
    for c in range(N_LEAF):
        s = map_ref[c, front] // N_FRONT
        for b in range(2):
            q = map_ref[c, leaf + b * N_LEAF] // N_FRONT * 2 + b - step * STEP_ROWS

            @pl.when((q >= 0) & (q < STEP_ROWS))
            def _():
                there = pl.ds(q * (8 * BLK) + s, BLK, stride=8)
                added = (late_ref if b else early_ref)[c].astype(F32)
                out_ref[there, :] = out_ref[there, :] + added

    @pl.when(front < KS)
    def _():
        column = pl.ds(pl.multiple_of(owner * BLK, BLK), BLK)
        for q, at in enumerate(order):
            out_ref[pl.ds(q * 8 * BLK, BLK, stride=8), :] = low_ref[at : at + BLK, column]

    @pl.when(step == 0)
    def _():
        out_ref[: 8 * BLK, :] = jnp.zeros((8 * BLK, BLK), F32)

        @pl.when(front < KS)
        def _():
            out_ref[pl.ds(0, BLK, stride=8), :] = l_ref[...]


def schur(child_map, low, given, early, panels, w, m, rows, front):
    steps = 16 // STEP_ROWS
    block = pl.BlockSpec((STEP_ROWS * BLK * 8, BLK), lambda i: (i, 0))
    return pl.pallas_call(
        schur_kernel,
        name="schur",
        grid=(steps,),
        out_shape=jax.ShapeDtypeStruct((16 * BLK * 8, BLK), F32),
        in_specs=[
            TABLE,
            WHOLE,
            pl.BlockSpec((N_LEAF, 1, BLK, BLK), lambda i: (0, 1, 0, 0)),
            WHOLE,
            WHOLE,
            WHOLE,
            pl.BlockSpec(memory_space=pltpu.HBM),
            pl.BlockSpec(memory_space=pltpu.HBM),
            block,
        ],
        out_specs=block,
        scratch_shapes=[
            pltpu.VMEM((ORDER, ORDER), BF16),
            pltpu.VMEM((2, ORDER, ORDER), BF16),
            pltpu.VMEM((2, KS, 2 * BLK, BLK), BF16),
            pltpu.VMEM((STEP_ROWS * BLK, ORDER), F32),
            pltpu.VMEM((N_LEAF, BLK, BLK), BF16),
            pltpu.SemaphoreType.DMA((16 // STEP_ROWS, 2 * KS)),
            pltpu.SemaphoreType.DMA((2, KS)),
            pltpu.SemaphoreType.DMA,
        ],
        compiler_params=pltpu.CompilerParams(vmem_limit_bytes=52 << 20),
    )(child_map, low, given, early, panels, w, m, rows, front)


def gather(x, axis, count):
    spread = jnp.broadcast_to(x[None], (count, *x.shape))
    return lax.all_to_all(spread, axis, 0, 0)


def exchange(flip):
    return [
        (a * N_FRONT + b * N_LEAF + c, c * N_FRONT + (b ^ flip) * N_LEAF + a)
        for a in range(N_LEAF)
        for b in range(2)
        for c in range(N_LEAF)
    ]


def front_pieces(first, leaf_id, front_id):
    z, x = front_id // 4, front_id % 4
    got = [
        lax.ppermute(first, "front", [(4 * i + j, (i + k) % 4 * 4 + j) for i in (0, 1) for j in range(4)])
        for k in (1, 2, 3)
    ]
    near = jnp.where(z == 0, first, jnp.where(z == 1, got[0], jnp.where(z == 2, got[1], got[2])))
    far = jnp.where(z == 0, got[2], jnp.where(z == 1, first, jnp.where(z == 2, got[0], got[1])))
    extra = jnp.where(leaf_id < 4, near[1], far[1])
    mine = jnp.stack([near[0], far[0], extra])
    every = [mine] + [
        lax.ppermute(mine, "front", [(4 * i + j, 4 * i + (j + k) % 4) for i in range(4) for j in range(4)])
        for k in (1, 2, 3)
    ]
    at = (x + 8 - leaf_id) % 4
    extra = every[0][2]
    for k in (1, 2, 3):
        extra = jnp.where(at == k, every[k][2], extra)
    return jnp.concatenate([one[:2] for one in every] + [extra[None]], axis=0)


def one_pass(front_entries, child_panels, child_blocks, child_map):
    front = front_entries.reshape(16 * BLK * 8, BLK)
    front_id = lax.axis_index("front")
    leaf_id = lax.axis_index("leaf")
    own = child_panels[0]
    halves_of = own.reshape(2, BLK // 2, own.shape[1])
    early = front_id < N_LEAF
    same = lax.ppermute(jnp.where(early, halves_of[0], halves_of[1]), MESH_AXES, exchange(0))
    other = lax.ppermute(jnp.where(early, halves_of[1], halves_of[0]), MESH_AXES, exchange(1))
    blocks = child_blocks[0].reshape(2, N_LEAF, BLK, BLK).transpose(1, 0, 2, 3)
    given = lax.all_to_all(blocks, "leaf", 0, 0)
    own, same, other, given = lax.optimization_barrier((own, same, other, given))
    panels = lax.all_gather(own, "leaf", axis=0)
    upper = gather(jnp.where(early, same, other), "front", N_FRONT)
    upper = upper.reshape(2, N_LEAF, BLK // 2, own.shape[1])
    lower = jnp.where(early, other, same).reshape(BLK // 2, 4, BLK).transpose(1, 0, 2)
    flat, turned, first = pivot_rows(child_map, front, given, upper, panels)
    cols = lax.all_gather(flat, "leaf", axis=0, tiled=True)
    turned = lax.ppermute(turned, MESH_AXES, exchange(0))
    whole = front_pieces(first, leaf_id, front_id)
    turned, whole = lax.optimization_barrier((turned, whole))
    across = [lax.ppermute(whole, "leaf", CORES)]
    along = [whole] + [
        lax.ppermute(whole, "leaf", [(i, (i + 2 * k) % N_LEAF) for i in range(N_LEAF)])
        for k in (1, 2, 3)
    ]
    across += [lax.ppermute(one, "leaf", CORES) for one in along[1:]]
    separator = along + across
    packed = jnp.concatenate([turned.reshape(ORDER, BLK), lower.reshape(2 * BLK, BLK)], axis=0)
    rows = lax.all_gather(packed, "front", axis=0)
    m, low = cholesky(separator)
    rows = rows.reshape(2, KS, ORDER + 2 * BLK, BLK)
    w, early_updates = columns(m, cols, given, upper, panels)
    out = schur(child_map, low, given, early_updates, panels, w, m, rows, front)
    return out.reshape(16, 1, BLK, 8, 1, BLK)


def solution(mesh):
    placed = (
        P(None, "leaf", None, None, "front", None),
        P("leaf", "front", None),
        P("leaf", None, "front"),
        P(),
    )
    return jax.shard_map(
        one_pass,
        mesh=mesh,
        in_specs=placed,
        out_specs=P(None, "leaf", None, None, "front", None),
        check_vma=False,
    )
```
